32 devices in a mesh: gx: 4 (over y, core), gy: 8 (over z, x).
Axes of the slice: x: 2, y: 2, z: 4, core: 2. Of those that a mesh axis runs over, the one named last changes fastest.
Arguments:
- right_side: float32 [64, 256, 128], P('gx', 'gy'), may hold values from -6 to 6
- first_guess: float32 [64, 256, 128], P('gx', 'gy'), may hold values from -6 to 6
- recycled: bfloat16 [8, 64, 256, 128], P(None, 'gx', 'gy'), may hold values from -4 to 4
- heights: int32 [64, 256], P('gx', 'gy'), may hold values from 0 to 64, as said below
- ground_codes: int32 [64, 256], P('gx', 'gy'), may hold values from 0 to 2
Outputs:
- solution: float32 [64, 256, 128], P('gx', 'gy')
- residual: float32 [64, 256, 128], P('gx', 'gy')
The draws below stay inside these ranges and needn't reach their ends.
Inputs may be any that keep to these rules, and one draw needn't show every extreme that they name: `heights`: height of the buildings standing in each column, 0 for open ground.
All inputs are finite; a program needn't handle non-finite values.
Results may differ from the reference program's by a relative error of at most 0.0003.
Values sent between devices are 32-bit elements; how exact they have to be, the bound alone decides.
A program may use at most 64 MiB of HBM per device.

```python
import jax
import jax.numpy as jnp
from jax import lax

NZ = 128
RECYCLE = 8
OUTER = 2
SWEEPS = 3
NX = 64
NY = 256


def basis_fields(key):
    noise = jax.random.normal(jax.random.fold_in(key, 31), (RECYCLE, NX, NY, NZ), jnp.float32)
    return jnp.clip(1.5 * noise, -4.0, 4.0)


def draw_recycled(key, part):
    return basis_fields(key).astype(jnp.bfloat16)


def draw_right_side(key, part):
    rough = jnp.clip(jax.random.normal(jax.random.fold_in(key, 5), (NX, NY, NZ), jnp.float32), -6.0, 6.0)
    sizes_key = jax.random.fold_in(key, 43)
    signs_key = jax.random.fold_in(key, 47)
    magnitude = jax.random.uniform(sizes_key, (RECYCLE,), jnp.float32, 0.25, 0.6)
    signs = jnp.where(jax.random.bernoulli(signs_key, 0.5, (RECYCLE,)), 1.0, -1.0)
    weights = magnitude * signs
    mixture = jnp.tensordot(weights, basis_fields(key), axes=1)
    return jnp.clip(rough + mixture, -6.0, 6.0)


def draw_heights(key, part):
    first_key, second_key = jax.random.split(jax.random.fold_in(key, 17))
    tall = jax.random.randint(first_key, (NX, NY), 1, NZ // 2 + 1)
    open_ground = jax.random.randint(second_key, (NX, NY), 0, 3) == 0
    result = jnp.where(open_ground, 0, tall).astype(jnp.int32)
    result = result.at[0, 0].set(NZ // 2)
    result = result.at[0, 1].set(0)
    return result


def touch_ends(values, own_key, smallest, top_value):
    longest = values.shape.index(max(values.shape))
    spots = []
    for shift in (0, 1):
        where = [jax.random.randint(jax.random.fold_in(own_key, axis), (), 0, length) for axis, length in enumerate(values.shape)]
        where[longest] = (where[longest] + shift) % values.shape[longest]
        spots.append(tuple(where))
    return values.at[spots[0]].set(smallest).at[spots[1]].set(top_value)


def level_of(key, extent, cuts, smallest, largest):
    gain, own = 1.0, jax.random.fold_in(key, 6)
    for position, blocks in cuts:
        steps = jnp.exp(jax.random.uniform(jax.random.fold_in(own, position), (blocks,), jnp.float32, smallest / len(cuts), largest / len(cuts)))
        gain = gain * jnp.repeat(steps, extent[position] // blocks).reshape([-1 if axis == position else 1 for axis in range(len(extent))])
    return gain


def normal_values(key, dims, width, reach, cuts=(), dtype=jnp.bfloat16):
    values = jax.random.normal(key, dims, jnp.float32) * width
    if len(cuts) > 0:
        values = level_of(key, dims, cuts, -0.22, 0.18) * values
    return jnp.clip(values, min=-reach, max=reach).astype(dtype)


def setup_inputs(seed: int = 0) -> dict:
    keys = jax.random.split(jax.random.key(seed), 6)
    return {
        "right_side": draw_right_side(jax.random.fold_in(keys[5], 71), 0),
        "first_guess": normal_values(keys[1], (NX, NY, NZ), 1.0, 6.0, ((0, 4), (1, 8)), jnp.float32),
        "recycled": draw_recycled(jax.random.fold_in(keys[5], 71), 0),
        "heights": draw_heights(jax.random.fold_in(keys[5], 71), 0),
        "ground_codes": touch_ends(jax.random.randint(keys[4], (NX, NY), 0, 3), jax.random.fold_in(keys[4], 1), 0, 2).astype(jnp.int32),
    }


cheb_center = 7.25
cheb_half = 6.75
cheb_sigma = 7.25 / 6.75

def coefficients(ground):
    level = lax.broadcasted_iota(jnp.int32, (1, 1, NZ), 2)
    height = ground[0][:, :, None]
    code_col = ground[1][:, :, None]
    inside = ground[2][:, :, None]
    fluid_mask = jnp.where((inside > 0) & (level >= height), 1.0, 0.0).astype(jnp.float32)
    bottom = jnp.where(code_col == 1, 0.5, 0.0) + jnp.where(code_col == 2, 2.0, 0.0)
    extra_diag = jnp.where(level == 0, bottom, 0.0) + jnp.where(level == NZ - 1, 1.0, 0.0)
    return (fluid_mask, extra_diag.astype(jnp.float32))

def shift_upper(arr):
    return jnp.concatenate([arr[..., 1:], jnp.zeros_like(arr[..., :1])], -1)

def shift_lower(arr):
    return jnp.concatenate([jnp.zeros_like(arr[..., :1]), arr[..., :-1]], -1)

def operate(field_wide, fluid_mask, extra_diag):
    rows_a = fluid_mask.shape[0] - 2
    rows_b = fluid_mask.shape[1] - 2
    center_fluid = fluid_mask[1:-1, 1:-1]
    center_extra = extra_diag[1:-1, 1:-1]
    center_value = field_wide[..., 1:-1, 1:-1, :]
    summed = jnp.zeros_like(center_value)
    for off_a, off_b in ((2, 1), (0, 1), (1, 2), (1, 0)):
        near_fluid = fluid_mask[off_a:off_a + rows_a, off_b:off_b + rows_b]
        near_value = field_wide[..., off_a:off_a + rows_a, off_b:off_b + rows_b, :]
        summed = summed + near_fluid * (center_value - near_value)
    summed = summed + shift_upper(center_fluid) * (center_value - shift_upper(center_value))
    summed = summed + shift_lower(center_fluid) * (center_value - shift_lower(center_value))
    return center_fluid * (summed + center_extra * center_value) + (1.0 - center_fluid) * center_value

def padded_rim(field):
    return jnp.pad(field, ((1, 1), (1, 1), (0, 0)))

def small_solve(factor, vector):
    inner = lax.linalg.triangular_solve(factor, vector[:, None], left_side=True, lower=True)
    outer = lax.linalg.triangular_solve(factor, inner, left_side=True, lower=True, transpose_a=True)
    return outer[:, 0]

def project(vectors, field):
    return jnp.einsum('kxyz,xyz->k', vectors, field, precision=lax.Precision.HIGHEST)

def combine(coeffs, vectors):

    def add_one(carry, pair):
        return (carry + pair[0] * pair[1].astype(jnp.float32), None)
    result, unused = lax.scan(add_one, jnp.zeros(vectors.shape[1:], jnp.float32), (coeffs, vectors))
    return result

def reference(right_side, first_guess, recycled, heights, ground_codes):
    ground = jnp.stack([heights, ground_codes, jnp.ones_like(heights)], 0)
    ground = jnp.pad(ground, ((0, 0), (1, 1), (1, 1)))
    fluid_mask, extra_diag = coefficients(ground)
    images = lax.map(lambda vector: operate(padded_rim(vector.astype(jnp.float32)), fluid_mask, extra_diag), recycled)
    residual = right_side - operate(padded_rim(first_guess), fluid_mask, extra_diag)
    gram_matrix = jnp.einsum('kxyz,jxyz->kj', images, images, precision=lax.Precision.HIGHEST)
    start_proj = project(images, residual)
    factor = jnp.linalg.cholesky(gram_matrix)
    coeffs = small_solve(factor, start_proj)
    solution = first_guess + combine(coeffs, recycled)
    residual = residual - combine(coeffs, images)
    for outer_index in range(OUTER):
        correction = jnp.zeros_like(residual)
        remainder = residual
        direction = residual / cheb_center
        ratio_now = 1.0 / cheb_sigma
        for sweep_index in range(SWEEPS):
            correction = correction + direction
            remainder = remainder - operate(padded_rim(direction), fluid_mask, extra_diag)
            if sweep_index + 1 < SWEEPS:
                ratio_next = 1.0 / (2.0 * cheb_sigma - ratio_now)
                direction = ratio_next * ratio_now * direction + 2.0 * ratio_next / cheb_half * remainder
                ratio_now = ratio_next
        image_step = residual - remainder
        coeffs = small_solve(factor, project(images, image_step))
        image_step = image_step - combine(coeffs, images)
        correction = correction - combine(coeffs, recycled)
        step_length = jnp.sum(image_step * residual) / jnp.sum(image_step * image_step)
        solution = solution + step_length * correction
        residual = residual - step_length * image_step
    return (solution, residual)
```

```python
import functools

import jax
import jax.numpy as jnp
from jax import lax
from jax.experimental import pallas as pl
from jax.experimental.pallas import tpu as pltpu
from jax.sharding import PartitionSpec as P

OUTER = 2
SWEEPS = 3
GHOST = SWEEPS

CENTER = 7.25
HALF = 6.75
SIGMA = 7.25 / 6.75

F32 = jnp.float32


def kernel(
    gxn, gyn, count, a, b,
    rs_hbm, fg_hbm, rec_hbm, h_hbm, code_hbm,
    sol_ref, res_ref,
    rs_ref, fg_ref, rec_ref, ground, near_ground,
    wide0, xsend0, ysend0, yrecv0, rwide, ysend, yrecv, csend, crecv,
    fwide, diag, uwide, dwide, rem, cbuf, img, psend, slots,
    in_sem, gs_sem, gr_sem, hs_sem, hr_sem, ds_sem, dr_sem, ps_sem, pr_sem,
):
    lanes = 128
    S = b + 16
    n = gxn * gyn
    nf = count + 1
    gx = lax.axis_index("gx")
    gy = lax.axis_index("gy")
    me = gx * gyn + gy

    def at_dev(i, j):
        return dict(device_id={"gx": i, "gy": j}, device_id_type=pl.DeviceIdType.MESH)

    loads = [
        pltpu.make_async_copy(h_hbm, ground.at[0], in_sem.at[0]),
        pltpu.make_async_copy(code_hbm, ground.at[1], in_sem.at[1]),
        pltpu.make_async_copy(fg_hbm, fg_ref, in_sem.at[2]),
        pltpu.make_async_copy(rs_hbm, rs_ref, in_sem.at[3]),
    ] + [pltpu.make_async_copy(rec_hbm.at[m], rec_ref.at[m], in_sem.at[4 + m]) for m in range(count)]
    for cp in loads:
        cp.start()

    barrier = pltpu.get_barrier_semaphore()

    def greet(t, _):
        peer = lax.rem(me + t, n)
        pl.semaphore_signal(barrier, inc=1, **at_dev(peer // gyn, lax.rem(peer, gyn)))
        return 0

    lax.fori_loop(1, n, greet, 0)

    def base0(x):
        return S * (x + 1) + 8

    def base(x):
        return S * (x + GHOST) + 8

    def span(x):
        return pl.ds(S * (x + GHOST), S)

    lane8 = lax.broadcasted_iota(jnp.int32, (8, lanes), 1)
    sub8 = lax.broadcasted_iota(jnp.int32, (8, lanes), 0)
    row1 = lax.broadcasted_iota(jnp.int32, (1, lanes), 1)

    steps = ((-1, 0), (1, 0), (0, -1), (0, 1), (-1, -1), (-1, 1), (1, -1), (1, 1))
    opposite = [steps.index((-i, -j)) for i, j in steps]
    have, peers = [], []
    for i, j in steps:
        ok = None
        for at, size, by in ((gx, gxn, i), (gy, gyn, j)):
            if by:
                one = at > 0 if by < 0 else at < size - 1
                ok = one if ok is None else jnp.logical_and(ok, one)
        have.append(ok)
        peers.append(at_dev(gx + i, gy + j))

    def ground_copy(s):
        return pltpu.make_async_remote_copy(
            src_ref=ground, dst_ref=near_ground.at[opposite[s]],
            send_sem=gs_sem.at[s], recv_sem=gr_sem.at[opposite[s]], **peers[s],
        )

    def field_copy(m, s):
        w = wide0.at[m]
        src = (
            xsend0.at[m, 0], xsend0.at[m, 1],
            ysend0.at[m, 0], ysend0.at[m, 1],
        )[s]
        dst = (
            w.at[pl.ds(base0(a), b), :], w.at[pl.ds(base0(-1), b), :],
            yrecv0.at[m, 1], yrecv0.at[m, 0],
        )[s]
        return pltpu.make_async_remote_copy(
            src_ref=src, dst_ref=dst,
            send_sem=hs_sem.at[m, s], recv_sem=hr_sem.at[m, opposite[s]], **peers[s],
        )

    def deep_copies(r, s):
        w = rwide.at[r]
        if s < 2:
            pieces = [
                (
                    w.at[pl.ds(base(i if s == 0 else a - GHOST + i), b), :],
                    w.at[pl.ds(base(a + i if s == 0 else i - GHOST), b), :],
                )
                for i in range(GHOST)
            ]
        elif s < 4:
            pieces = [(ysend.at[r, s - 2], yrecv.at[r, 3 - s])]
        else:
            pieces = [(csend.at[r, s - 4], crecv.at[r, opposite[s] - 4])]
        return [
            pltpu.make_async_remote_copy(
                src_ref=p, dst_ref=q,
                send_sem=ds_sem.at[r, s, i], recv_sem=dr_sem.at[r, opposite[s], i], **peers[s],
            )
            for i, (p, q) in enumerate(pieces)
        ]

    def each(sides, act):
        for s in sides:
            @pl.when(have[s])
            def _(s=s):
                act(s)

    def all_do(cps, what):
        for cp in cps:
            getattr(cp, what)()

    zeros = jnp.zeros((b, lanes), F32)
    for s in range(8):
        @pl.when(jnp.logical_not(have[s]))
        def _(s=s):
            near_ground[s, 0] = jnp.full((a, b), 255, jnp.int32)
            near_ground[s, 1] = jnp.zeros((a, b), jnp.int32)
            if s < 2:
                for m in range(nf):
                    wide0[m, pl.ds(base0(-1 if s == 0 else a), b), :] = zeros
                for r in range(OUTER):
                    for i in range(GHOST):
                        rwide[r, pl.ds(base(i - GHOST if s == 0 else a + i), b), :] = zeros
            elif s < 4:
                for m in range(nf):
                    yrecv0[m, s - 2] = jnp.zeros((a, lanes), F32)
                for r in range(OUTER):
                    for i in range(GHOST):
                        yrecv[r, s - 2, i] = jnp.zeros((a, lanes), F32)
            else:
                for r in range(OUTER):
                    for i in range(3):
                        crecv[r, s - 4, i] = jnp.zeros((1, lanes), F32)

    ones = jnp.ones((b, lanes), jnp.bfloat16)
    yi = lax.broadcasted_iota(jnp.int32, (S, b), 0)
    ji = lax.broadcasted_iota(jnp.int32, (S, b), 1)
    lane_f = lax.broadcasted_iota(jnp.int32, (S, lanes), 1).astype(F32)
    lane_s = lax.broadcasted_iota(jnp.int32, (S, lanes), 1)

    def spread(tables, i):
        left, mid, right = [jnp.broadcast_to(t[i : i + 1, :].astype(F32), (S, b)) for t in tables]
        pick = jnp.where(yi - 8 == ji, mid, 0.0)
        pick = jnp.where(yi == ji - (b - 8), left, pick)
        pick = jnp.where(yi - (b + 8) == ji, right, pick)
        return jnp.dot(pick.astype(jnp.bfloat16), ones, preferred_element_type=F32)

    def mask_row(x, trio, i):
        high = spread([t.at[0] for t in trio], i)
        code = spread([t.at[1] for t in trio], i)
        fwide[span(x), :] = jnp.where(lane_f >= high, 1.0, 0.0)
        bottom = jnp.where(code == 1.0, 0.5, 0.0) + jnp.where(code == 2.0, 2.0, 0.0)
        diag[span(x), :] = jnp.where(lane_s == 0, bottom, 0.0) + jnp.where(
            lane_s == lanes - 1, 1.0, 0.0
        )

    def fluid(x):
        return fwide[pl.ds(base(x), b), :]

    def prepare(m):
        loads[2 if m == count else 4 + m].wait()
        w = wide0.at[m]
        for x in range(a):
            rows = slice(x * b, x * b + b)
            v = fg_ref[rows, :] if m == count else rec_ref[m, rows, :].astype(F32)
            w[pl.ds(base0(x), b), :] = v
            if x == 0:
                xsend0[m, 0] = v
            if x == a - 1:
                xsend0[m, 1] = v
        ysend0[m, 0] = w[pl.ds(S + 8, a, stride=S), :]
        ysend0[m, 1] = w[pl.ds(S + 8 + b - 1, a, stride=S), :]

    order = [count] + list(range(count))
    early = order[: (nf + 1) // 2]
    for m in early:
        prepare(m)
    all_do(loads[:2], "wait")
    pl.semaphore_wait(barrier, n - 1)
    each((4, 5, 6, 7, 2, 3, 0, 1), lambda s: ground_copy(s).start())
    for m in early:
        each((2, 3, 0, 1), lambda s: field_copy(m, s).start())
    for m in order[len(early) :]:
        prepare(m)
        each((2, 3, 0, 1), lambda s: field_copy(m, s).start())

    for x in range(a):
        mask_row(x, (ground,) * 3, x)

    @pl.loop(0, nf)
    def _(m):
        for x in range(a):
            at = pl.ds(base0(x), b)
            wide0[m, at, :] = fluid(x) * wide0[m, at, :]

    each(range(8), lambda s: ground_copy(opposite[s]).wait_recv())
    for x in range(-GHOST, a + GHOST):
        if x < 0:
            trio, i = (near_ground.at[4], near_ground.at[0], near_ground.at[5]), a + x
        elif x < a:
            trio, i = (near_ground.at[2], ground, near_ground.at[3]), x
        else:
            trio, i = (near_ground.at[6], near_ground.at[1], near_ground.at[7]), x - a
        mask_row(x, trio, i)

    def near(w, at, size):
        c = w[pl.ds(at, size), :]
        lane = lax.broadcasted_iota(jnp.int32, (size, lanes), 1)
        up = jnp.where(lane == lanes - 1, 0.0, pltpu.roll(c, lanes - 1, 1))
        down = jnp.where(lane == 0, 0.0, pltpu.roll(c, 1, 1))
        return (
            (w[pl.ds(at + S, size), :] + w[pl.ds(at - S, size), :])
            + (w[pl.ds(at + 1, size), :] + w[pl.ds(at - 1, size), :])
            + (up + down)
        )

    for x in range(1 - GHOST, a + GHOST - 1):
        f = fwide[span(x), :]
        diag[span(x), :] = f * (near(fwide, S * (x + GHOST), S) + diag[span(x), :]) + (1.0 - f)

    def arrive(m):
        each(range(4), lambda s: field_copy(m, opposite[s]).wait_recv())
        w = wide0.at[m]
        for x in (-1, a):
            at = pl.ds(base0(x), b)
            w[at, :] = fluid(x) * w[at, :]
        for i, x in enumerate((-1, b)):
            w[pl.ds(base0(0) + x, a, stride=S), :] = (
                fwide[pl.ds(base(0) + x, a, stride=S), :] * yrecv0[m, i]
            )

    def total(v):
        out = v[0:8]
        for i in range(8, b, 8):
            out = out + v[i : i + 8]
        return out

    zero8 = jnp.zeros((8, lanes), F32)
    table = {}
    loads[3].wait()
    for m in order:
        arrive(m)
        sums = [zero8] * (m + 2)
        for x in range(a):
            rows = slice(x * b, x * b + b)
            dg = diag[pl.ds(base(x), b), :]
            flow = fluid(x) * near(wide0.at[m], base0(x), b)
            if m == count:
                res_ref[rows, :] = rs_ref[rows, :] - (dg * fg_ref[rows, :] - flow)
                continue
            v = dg * rec_ref[m, rows, :].astype(F32) - flow
            img[m, rows, :] = v
            others = [img[q, rows, :] for q in range(m)] + [v, res_ref[rows, :]]
            sums = [acc + total(v * o) for acc, o in zip(sums, others)]
        if m < count:
            for q in range(m + 1):
                table[(q, m)] = sums[q]
            table[m] = sums[m + 1]

    def column(items):
        rows = [jnp.sum(v, axis=0, keepdims=True) for v in items]
        if len(rows) < 8:
            rows.append(jnp.zeros((8 - len(rows), lanes), F32))
        return jnp.sum(jnp.concatenate(rows, axis=0), axis=1, keepdims=True)

    packed = zero8
    for q in range(count + 1):
        items = (
            [table[(min(m, q), max(m, q))] for m in range(count)]
            if q < count
            else [table[m] for m in range(count)]
        )
        packed = packed + jnp.where(lane8 == 16 * sub8 + q, column(items), 0.0)

    gis = [lax.rem(gx + i, gxn) for i in range(gxn)]
    gjs = [lax.rem(gy + j, gyn) for j in range(gyn)]
    far_first = sorted(
        [(i, j) for i in range(gxn) for j in range(gyn) if i or j],
        key=lambda t: (abs(t[1] - gyn // 2), abs(t[0] - gxn // 2)),
    )

    def all_sum(k, row):
        psend[k] = row
        slots[k, me] = row

        def send(gi, gj):
            pltpu.make_async_remote_copy(
                src_ref=psend.at[k], dst_ref=slots.at[k, me],
                send_sem=ps_sem.at[k], recv_sem=pr_sem.at[k], **at_dev(gi, gj),
            ).start()

        if n <= 64:
            for i, j in far_first:
                send(gis[i], gjs[j])
        else:
            def step(t, _):
                peer = lax.rem(me + t, n)
                send(peer // gyn, lax.rem(peer, gyn))
                return 0

            lax.fori_loop(1, n, step, 0)
        most = slots.at[k, pl.ds(0, n - 1)]
        pltpu.make_async_copy(most, most, pr_sem.at[k]).wait()
        out = jnp.sum(slots[k], axis=0)
        return out

    row = all_sum(0, jnp.sum(packed, axis=0, keepdims=True))

    wrow = jnp.broadcast_to(row, (8, lanes))
    mat = zero8
    for m in range(count):
        moved = wrow if m == 0 else pltpu.roll(wrow, lanes - 16 * m, 1)
        mat = jnp.where(sub8 == m, moved, mat)
    mat = jnp.where(lane8 <= count, mat, 0.0) + jnp.where(lane8 == 16 + sub8, 1.0, 0.0)
    for k in range(count):
        pivot = mat[k : k + 1, :] / mat[k : k + 1, k : k + 1]
        mat = jnp.where(sub8 == k, pivot, mat - mat[:, k : k + 1] * pivot)
    inverse = pltpu.roll(mat, lanes - 16, 1)

    def whole(v):
        return jnp.concatenate([jnp.broadcast_to(v, (8, lanes))] * (b // 8), axis=0)

    coeffs = [whole(mat[m : m + 1, count : count + 1]) for m in range(count)]

    for x in range(a):
        rows = slice(x * b, x * b + b)
        res = res_ref[rows, :]
        for m in range(count):
            res = res - coeffs[m] * img[m, rows, :]
        rwide[0, pl.ds(base(x), b), :] = res

    def first_solution(x):
        rows = slice(x * b, x * b + b)
        sol = fg_ref[rows, :]
        for m in range(count):
            sol = sol + coeffs[m] * rec_ref[m, rows, :].astype(F32)
        sol_ref[rows, :] = sol

    later = first_solution

    bits = ((0, 0), (0, 1), (1, 0))

    for outer in range(OUTER):
        w = rwide.at[outer]
        for i in range(GHOST):
            ysend[outer, 0, i] = w[pl.ds(base(0) + i, a, stride=S), :]
            ysend[outer, 1, i] = w[pl.ds(base(0) + b - 1 - i, a, stride=S), :]
        for s in range(4, 8):
            for i, (p, q) in enumerate(bits):
                x = p if steps[s][0] < 0 else a - 1 - p
                y = q if steps[s][1] < 0 else b - 1 - q
                csend[outer, s - 4, i] = w[pl.ds(base(x) + y, 1), :]
        each((4, 5, 6, 7, 2, 3, 0, 1), lambda s: all_do(deep_copies(outer, s), "start"))
        for x in range(a):
            later(x)

        accs = [zero8] * count
        for x in range(a):
            rows = slice(x * b, x * b + b)
            res = w[pl.ds(base(x), b), :]
            accs = [acc + total(img[m, rows, :] * res) for m, acc in enumerate(accs)]
        alongs = column(accs)
        each(range(8), lambda s: all_do(deep_copies(outer, opposite[s]), "wait_recv"))
        for i in range(GHOST):
            w[pl.ds(base(0) - 1 - i, a, stride=S), :] = yrecv[outer, 0, i]
            w[pl.ds(base(0) + b + i, a, stride=S), :] = yrecv[outer, 1, i]
        for s in range(4, 8):
            for i, (p, q) in enumerate(bits):
                x = -1 - p if steps[s][0] < 0 else a + p
                y = -1 - q if steps[s][1] < 0 else b + q
                w[pl.ds(base(x) + y, 1), :] = crecv[outer, s - 4, i]
        for x in range(-GHOST, a + GHOST):
            uwide[0, span(x), :] = fwide[span(x), :] * (w[span(x), :] * (1.0 / CENTER))
        rho = 1.0 / SIGMA
        for sweep in range(SWEEPS):
            rho_new = 1.0 / (2.0 * SIGMA - rho)
            grow = SWEEPS - 1 - sweep
            for x in range(-grow, a + grow):
                at, size = (base(x), b) if grow == 0 else (S * (x + GHOST), S)
                rows = pl.ds(at, size)
                f = fwide[rows, :]
                old = w[rows, :] if sweep == 0 else rem[rows, :]
                d = old * (1.0 / CENTER) if sweep == 0 else dwide[rows, :]
                left = old - (diag[rows, :] * d - f * near(uwide.at[sweep], at, size))
                cbuf[rows, :] = d if sweep == 0 else cbuf[rows, :] + d
                rem[rows, :] = left
                if sweep + 1 < SWEEPS:
                    d = (rho_new * rho) * d + (2.0 * rho_new / HALF) * left
                    dwide[rows, :] = d
                    uwide[sweep + 1, rows, :] = f * d
            rho = rho_new

        accs = [zero8] * (count + 2)
        for x in range(a):
            rows = slice(x * b, x * b + b)
            at = pl.ds(base(x), b)
            res = rwide[outer, at, :]
            image = res - rem[at, :]
            others = [img[m, rows, :] for m in range(count)] + [res, image]
            accs = [acc + total(image * o) for acc, o in zip(accs, others)]
        packed = (
            jnp.where(lane8 == sub8, column(accs[:count]), 0.0)
            + jnp.where(lane8 == sub8 + 8, alongs, 0.0)
            + jnp.where(lane8 == sub8 + 16, column(accs[count:]), 0.0)
        )
        row = all_sum(1 + outer, jnp.sum(packed, axis=0, keepdims=True))
        onto = jnp.sum(jnp.where(lane8 == sub8, jnp.broadcast_to(row, (8, lanes)), 0.0), axis=1, keepdims=True)
        y = jnp.sum(onto * inverse, axis=0, keepdims=True)
        y = jnp.where(row1 < count, y, 0.0)
        along = pltpu.roll(jnp.broadcast_to(row, (8, lanes)), lanes - 8, 1)[0:1]
        numerator = row[:, 16:17] - jnp.sum(y * along, axis=1, keepdims=True)
        denominator = row[:, 17:18] - jnp.sum(y * row, axis=1, keepdims=True)
        step = whole(numerator / denominator)
        ys = [whole(y[:, m : m + 1]) for m in range(count)]

        for x in range(a):
            rows = slice(x * b, x * b + b)
            at = pl.ds(base(x), b)
            res = rwide[outer, at, :]
            image = res - rem[at, :]
            for m in range(count):
                image = image - ys[m] * img[m, rows, :]
            res = res - step * image
            if outer + 1 < OUTER:
                rwide[outer + 1, at, :] = res
            else:
                res_ref[rows, :] = res

        def solution_update(x, step=step, ys=ys):
            rows = slice(x * b, x * b + b)
            c = cbuf[pl.ds(base(x), b), :]
            for m in range(count):
                c = c - ys[m] * rec_ref[m, rows, :].astype(F32)
            sol_ref[rows, :] = sol_ref[rows, :] + step * c

        later = solution_update

    for x in range(a):
        later(x)

    for k in range(OUTER + 1):
        most = slots.at[k, pl.ds(0, n - 1)]
        pltpu.make_async_copy(most, most, ps_sem.at[k]).wait()
    each(range(8), lambda s: ground_copy(s).wait_send())
    for m in range(nf):
        each(range(4), lambda s: field_copy(m, s).wait_send())
    for r in range(OUTER):
        each(range(8), lambda s: all_do(deep_copies(r, s), "wait_send"))


def store(sol_ref, res_ref, sol_out, res_out, sem):
    cps = [
        pltpu.make_async_copy(sol_ref, sol_out, sem.at[0]),
        pltpu.make_async_copy(res_ref, res_out, sem.at[1]),
    ]
    for cp in cps:
        cp.start()
    for cp in cps:
        cp.wait()


def solution(mesh):
    gxn, gyn = mesh.shape["gx"], mesh.shape["gy"]

    def local(right_side, first_guess, recycled, heights, ground_codes):
        a, b, nz = right_side.shape
        count = recycled.shape[0]
        field = jax.ShapeDtypeStruct((a * b, nz), F32)
        vm = pl.BlockSpec(memory_space=pltpu.VMEM)
        wide_f = pltpu.VMEM(((a + 2 * GHOST) * (b + 16), nz), F32)
        n = gxn * gyn
        hbm = pl.BlockSpec(memory_space=pltpu.HBM)
        dma = pltpu.SemaphoreType.DMA
        sol, res = pl.pallas_call(
            functools.partial(kernel, gxn, gyn, count, a, b),
            out_shape=(field, field),
            in_specs=[hbm] * 5,
            out_specs=(vm, vm),
            scratch_shapes=[
                pltpu.VMEM((a * b, nz), F32),
                pltpu.VMEM((a * b, nz), F32),
                pltpu.VMEM((count, a * b, nz), jnp.bfloat16),
                pltpu.VMEM((2, a, b), jnp.int32),
                pltpu.VMEM((8, 2, a, b), jnp.int32),
                pltpu.VMEM((count + 1, (a + 2) * (b + 16), nz), F32),
                pltpu.VMEM((count + 1, 2, b, nz), F32),
                pltpu.VMEM((count + 1, 2, a, nz), F32),
                pltpu.VMEM((count + 1, 2, a, nz), F32),
                pltpu.VMEM((OUTER,) + wide_f.shape, F32),
                pltpu.VMEM((OUTER, 2, GHOST, a, nz), F32),
                pltpu.VMEM((OUTER, 2, GHOST, a, nz), F32),
                pltpu.VMEM((OUTER, 4, 3, 1, nz), F32),
                pltpu.VMEM((OUTER, 4, 3, 1, nz), F32),
                wide_f,
                wide_f,
                pltpu.VMEM((SWEEPS,) + wide_f.shape, F32),
                wide_f,
                wide_f,
                wide_f,
                pltpu.VMEM((count, a * b, nz), F32),
                pltpu.VMEM((OUTER + 1, 1, nz), F32),
                pltpu.VMEM((OUTER + 1, n, 1, nz), F32),
                dma((4 + count,)),
                dma((8,)),
                dma((8,)),
                dma((count + 1, 4)),
                dma((count + 1, 4)),
                dma((OUTER, 8, GHOST)),
                dma((OUTER, 8, GHOST)),
                dma((OUTER + 1,)),
                dma((OUTER + 1,)),
            ],
            compiler_params=pltpu.CompilerParams(
                collective_id=0, has_side_effects=True, vmem_limit_bytes=32 * 2**20
            ),
        )(*[
            pltpu.with_memory_space_constraint(v, pltpu.HBM)
            for v in (
                right_side.reshape(a * b, nz),
                first_guess.reshape(a * b, nz),
                recycled.reshape(count, a * b, nz),
                heights,
                ground_codes,
            )
        ])
        sol, res = pl.pallas_call(
            store,
            out_shape=(field, field),
            in_specs=[vm] * 2,
            out_specs=(hbm, hbm),
            scratch_shapes=[dma((2,))],
            compiler_params=pltpu.CompilerParams(vmem_limit_bytes=4 * 2**20),
        )(sol, res)
        return sol.reshape(a, b, nz), res.reshape(a, b, nz)

    placed = (
        P("gx", "gy", None),
        P("gx", "gy", None),
        P(None, "gx", "gy", None),
        P("gx", "gy"),
        P("gx", "gy"),
    )
    return jax.shard_map(
        local,
        mesh=mesh,
        in_specs=placed,
        out_specs=(P("gx", "gy", None), P("gx", "gy", None)),
        check_vma=False,
    )
```

```python
import functools

import jax
import jax.numpy as jnp
from jax import lax
from jax.experimental import pallas as pl
from jax.experimental.pallas import tpu as pltpu
from jax.sharding import PartitionSpec as P

OUTER = 2
SWEEPS = 3
GHOST = SWEEPS
NEAR = 2

CENTER = 7.25
HALF = 6.75
SIGMA = 7.25 / 6.75

F32 = jnp.float32


def kernel(
    gxn, gyn, count, a, b,
    rs_hbm, fg_hbm, rec_hbm, h_hbm, code_hbm,
    sol_ref, res_ref,
    rs_ref, fg_ref, rec_ref, ground, near_ground,
    wide0, xrecv0, ysend0, yrecv0, rwide, ysend, yrecv, csend, crecv,
    fwide, diag, uwide, dwide, rem, cbuf, img, psend, slots,
    in_sem, gs_sem, gr_sem, hs_sem, hr_sem, ds_sem, dr_sem, ps_sem, pr_sem, known,
):
    lanes = 128
    S = b + 16
    n = gxn * gyn
    nf = count + 1
    gx = lax.axis_index("gx")
    gy = lax.axis_index("gy")
    me = gx * gyn + gy

    def at_dev(i, j):
        return dict(device_id={"gx": i, "gy": j}, device_id_type=pl.DeviceIdType.MESH)

    loads = [
        pltpu.make_async_copy(h_hbm, ground.at[0], in_sem.at[0]),
        pltpu.make_async_copy(code_hbm, ground.at[1], in_sem.at[1]),
        pltpu.make_async_copy(fg_hbm, fg_ref, in_sem.at[2]),
        pltpu.make_async_copy(rs_hbm, rs_ref, in_sem.at[3]),
    ] + [pltpu.make_async_copy(rec_hbm.at[m], rec_ref.at[m], in_sem.at[4 + m]) for m in range(count)]
    for cp in loads:
        cp.start()

    barrier = pltpu.get_barrier_semaphore()

    gis = [lax.rem(gx + i, gxn) for i in range(gxn)]
    gjs = [lax.rem(gy + j, gyn) for j in range(gyn)]

    greeters = -1
    for j in sorted(range(-NEAR, NEAR + 1), key=abs):
        inside = jnp.logical_and(gy + j >= 0, gy + j < gyn)
        greeters = greeters + jnp.where(inside, gxn, 0)

        @pl.when(inside)
        def _(j=j):
            for i in range(gxn):
                if i or j:
                    pl.semaphore_signal(barrier, inc=1, **at_dev(gis[i], gy + j))

    stages, reach = [], NEAR
    while reach < gyn - 1:
        stages.append(reach)
        reach *= 2

    def stage(k, act):
        for side, j in enumerate((-stages[k], stages[k])):
            @pl.when(jnp.logical_and(gy + j >= 0, gy + j < gyn))
            def _(side=side, j=j):
                if act == "signal":
                    pl.semaphore_signal(known.at[k, 1 - side], inc=1, **at_dev(gx, gy + j))
                else:
                    pl.semaphore_wait(known.at[k, side], 1)

    def base0(x):
        return S * (x + 1) + 8

    def base(x):
        return S * (x + GHOST) + 8

    def span(x):
        return pl.ds(S * (x + GHOST), S)

    lane8 = lax.broadcasted_iota(jnp.int32, (8, lanes), 1)
    sub8 = lax.broadcasted_iota(jnp.int32, (8, lanes), 0)
    row1 = lax.broadcasted_iota(jnp.int32, (1, lanes), 1)

    steps = ((-1, 0), (1, 0), (0, -1), (0, 1), (-1, -1), (-1, 1), (1, -1), (1, 1))
    opposite = [steps.index((-i, -j)) for i, j in steps]
    have, peers = [], []
    for i, j in steps:
        ok = None
        for at, size, by in ((gx, gxn, i), (gy, gyn, j)):
            if by:
                one = at > 0 if by < 0 else at < size - 1
                ok = one if ok is None else jnp.logical_and(ok, one)
        have.append(ok)
        peers.append(at_dev(gx + i, gy + j))

    def ground_copy(s):
        return pltpu.make_async_remote_copy(
            src_ref=ground, dst_ref=near_ground.at[opposite[s]],
            send_sem=gs_sem.at[s], recv_sem=gr_sem.at[opposite[s]], **peers[s],
        )

    def field_copy(m, s):
        w = wide0.at[m]
        src = (
            w.at[pl.ds(base0(0), b), :], w.at[pl.ds(base0(a - 1), b), :],
            ysend0.at[m, 0], ysend0.at[m, 1],
        )[s]
        dst = (
            xrecv0.at[m, 1], xrecv0.at[m, 0],
            yrecv0.at[m, 1], yrecv0.at[m, 0],
        )[s]
        return pltpu.make_async_remote_copy(
            src_ref=src, dst_ref=dst,
            send_sem=hs_sem.at[m, s], recv_sem=hr_sem.at[m, opposite[s]], **peers[s],
        )

    def deep_copies(r, s):
        w = rwide.at[r]
        if s < 2:
            pieces = [
                (
                    w.at[pl.ds(base(i if s == 0 else a - GHOST + i), b), :],
                    w.at[pl.ds(base(a + i if s == 0 else i - GHOST), b), :],
                )
                for i in range(GHOST)
            ]
        elif s < 4:
            pieces = [(ysend.at[r, s - 2], yrecv.at[r, 3 - s])]
        else:
            pieces = [(csend.at[r, s - 4], crecv.at[r, opposite[s] - 4])]
        return [
            pltpu.make_async_remote_copy(
                src_ref=p, dst_ref=q,
                send_sem=ds_sem.at[r, s, i], recv_sem=dr_sem.at[r, opposite[s], i], **peers[s],
            )
            for i, (p, q) in enumerate(pieces)
        ]

    def each(sides, act):
        for s in sides:
            @pl.when(have[s])
            def _(s=s):
                act(s)

    def all_do(cps, what):
        for cp in cps:
            getattr(cp, what)()

    zeros = jnp.zeros((b, lanes), F32)
    for s in range(8):
        @pl.when(jnp.logical_not(have[s]))
        def _(s=s):
            near_ground[s, 0] = jnp.full((a, b), 255, jnp.int32)
            near_ground[s, 1] = jnp.zeros((a, b), jnp.int32)
            if s < 2:
                for m in range(nf):
                    xrecv0[m, s] = zeros
                for r in range(OUTER):
                    for i in range(GHOST):
                        rwide[r, pl.ds(base(i - GHOST if s == 0 else a + i), b), :] = zeros
            elif s < 4:
                for m in range(nf):
                    yrecv0[m, s - 2] = jnp.zeros((a, lanes), F32)
                for r in range(OUTER):
                    for i in range(GHOST):
                        yrecv[r, s - 2, i] = jnp.zeros((a, lanes), F32)
            else:
                for r in range(OUTER):
                    for i in range(3):
                        crecv[r, s - 4, i] = jnp.zeros((1, lanes), F32)

    ones = jnp.ones((b, lanes), jnp.bfloat16)
    yi = lax.broadcasted_iota(jnp.int32, (S, b), 0)
    ji = lax.broadcasted_iota(jnp.int32, (S, b), 1)
    lane_f = lax.broadcasted_iota(jnp.int32, (S, lanes), 1).astype(F32)
    lane_s = lax.broadcasted_iota(jnp.int32, (S, lanes), 1)

    def spread(tables, i):
        left, mid, right = [jnp.broadcast_to(t[i : i + 1, :].astype(F32), (S, b)) for t in tables]
        pick = jnp.where(yi - 8 == ji, mid, 0.0)
        pick = jnp.where(yi == ji - (b - 8), left, pick)
        pick = jnp.where(yi - (b + 8) == ji, right, pick)
        return jnp.dot(pick.astype(jnp.bfloat16), ones, preferred_element_type=F32)

    def mask_row(x, trio, i):
        high = spread([t.at[0] for t in trio], i)
        code = spread([t.at[1] for t in trio], i)
        fwide[span(x), :] = jnp.where(lane_f >= high, 1.0, 0.0)
        bottom = jnp.where(code == 1.0, 0.5, 0.0) + jnp.where(code == 2.0, 2.0, 0.0)
        diag[span(x), :] = jnp.where(lane_s == 0, bottom, 0.0) + jnp.where(
            lane_s == lanes - 1, 1.0, 0.0
        )

    def fluid(x):
        return fwide[pl.ds(base(x), b), :]

    own_y = jnp.logical_and(lax.broadcasted_iota(jnp.int32, (S, lanes), 0) >= 8,
                            lax.broadcasted_iota(jnp.int32, (S, lanes), 0) < b + 8)

    def near(w, at, size):
        c = w[pl.ds(at, size), :]
        lane = lax.broadcasted_iota(jnp.int32, (size, lanes), 1)
        up = jnp.where(lane == lanes - 1, 0.0, pltpu.roll(c, lanes - 1, 1))
        down = jnp.where(lane == 0, 0.0, pltpu.roll(c, 1, 1))
        return (
            (w[pl.ds(at + S, size), :] + w[pl.ds(at - S, size), :])
            + (w[pl.ds(at + 1, size), :] + w[pl.ds(at - 1, size), :])
            + (up + down)
        )

    all_do(loads[:2], "wait")
    for x in (-1, a):
        fwide[span(x), :] = jnp.zeros((S, lanes), F32)
    for x in range(a):
        mask_row(x, (ground,) * 3, x)
        fwide[span(x), :] = jnp.where(own_y, fwide[span(x), :], 0.0)

    def set_diag(x):
        f = fwide[span(x), :]
        diag[span(x), :] = f * (near(fwide, S * (x + GHOST), S) + diag[span(x), :]) + (1.0 - f)

    def prepare(m):
        loads[2 if m == count else 4 + m].wait()
        w = wide0.at[m]
        for x in range(a):
            rows = slice(x * b, x * b + b)
            v = fg_ref[rows, :] if m == count else rec_ref[m, rows, :].astype(F32)
            w[pl.ds(base0(x), b), :] = fluid(x) * v
        ysend0[m, 0] = w[pl.ds(S + 8, a, stride=S), :]
        ysend0[m, 1] = w[pl.ds(S + 8 + b - 1, a, stride=S), :]

    order = [count] + list(range(count))
    early = order[: (nf + 1) // 2]
    for m in early:
        prepare(m)
    pl.semaphore_wait(barrier, greeters)
    each((4, 5, 6, 7, 2, 3, 0, 1), lambda s: ground_copy(s).start())
    for m in early:
        each((2, 3, 0, 1), lambda s: field_copy(m, s).start())
    for k in range(len(stages)):
        if k == 0:
            stage(k, "signal")
    for m in order[len(early) :]:
        prepare(m)
        each((2, 3, 0, 1), lambda s: field_copy(m, s).start())

    zeros_a = jnp.zeros((a, lanes), F32)
    for m in range(nf):
        w = wide0.at[m]
        for x in (-1, a):
            w[pl.ds(base0(x), b), :] = zeros
        for y in (-1, b):
            w[pl.ds(base0(0) + y, a, stride=S), :] = zeros_a
    for x in range(a):
        set_diag(x)

    zero8 = jnp.zeros((8, lanes), F32)

    def tiles(v):
        return [v[i : i + 8] for i in range(0, v.shape[0], 8)]

    def total(v):
        return functools.reduce(jnp.add, tiles(v))

    table = {}
    loads[3].wait()
    waited = 0
    for turn, m in enumerate(order):
        sums = [zero8] * (m + 2)
        for x in range(a):
            rows = slice(x * b, x * b + b)
            dg = diag[pl.ds(base(x), b), :]
            flow = fluid(x) * near(wide0.at[m], base0(x), b)
            if m == count:
                res_ref[rows, :] = rs_ref[rows, :] - (dg * fg_ref[rows, :] - flow)
                continue
            v = dg * rec_ref[m, rows, :].astype(F32) - flow
            img[m, rows, :] = v
            if 0 < x < a - 1:
                inner = tiles(v)
                inner[0] = jnp.where(sub8 > 0, inner[0], 0.0)
                inner[-1] = jnp.where(sub8 < 7, inner[-1], 0.0)
                others = [img[q, rows, :] for q in range(m)] + [v, res_ref[rows, :]]
                sums = [
                    acc + functools.reduce(jnp.add, [i * j for i, j in zip(inner, tiles(o))])
                    for acc, o in zip(sums, others)
                ]
        if m < count:
            table[m] = sums
        if turn in (2, 6) and waited < len(stages):
            stage(waited, "wait")
            waited += 1
            if waited < len(stages):
                stage(waited, "signal")
    while waited < len(stages):
        stage(waited, "wait")
        waited += 1
        if waited < len(stages):
            stage(waited, "signal")

    each(range(8), lambda s: ground_copy(opposite[s]).wait_recv())
    for x in range(-GHOST, a + GHOST):
        if x < 0:
            trio, i = (near_ground.at[4], near_ground.at[0], near_ground.at[5]), a + x
        elif x < a:
            trio, i = (near_ground.at[2], ground, near_ground.at[3]), x
        else:
            trio, i = (near_ground.at[6], near_ground.at[1], near_ground.at[7]), x - a
        mask_row(x, trio, i)

    for x in range(1 - GHOST, a + GHOST - 1):
        set_diag(x)

    def column(items):
        rows = [jnp.sum(v, axis=0, keepdims=True) for v in items]
        if len(rows) < 8:
            rows.append(jnp.zeros((8 - len(rows), lanes), F32))
        return jnp.sum(jnp.concatenate(rows, axis=0), axis=1, keepdims=True)

    sub_a = lax.broadcasted_iota(jnp.int32, (a, lanes), 0)
    mid_a = jnp.logical_and(sub_a > 0, sub_a < a - 1)
    ends = [slice(x * b, x * b + b) for x in (0, a - 1)]
    strips = [pl.ds(y, a, stride=b) for y in (0, b - 1)]
    packed = zero8
    starts = []
    for m in order:
        each(range(4), lambda s: field_copy(m, opposite[s]).wait_recv())
        out = res_ref if m == count else img.at[m]
        sign = -1.0 if m == count else 1.0
        for i, (x, g) in enumerate(((0, -1), (a - 1, a))):
            add = fluid(g) * wide0[m, pl.ds(base0(x), b), :] - fluid(x) * xrecv0[m, i]
            out[ends[i], :] = out[ends[i], :] + sign * add
        for i, (y, g) in enumerate(((0, -1), (b - 1, b))):
            f_out = fwide[pl.ds(base(0) + g, a, stride=S), :]
            f_own = fwide[pl.ds(base(0) + y, a, stride=S), :]
            add = f_out * ysend0[m, i] - f_own * yrecv0[m, i]
            out[strips[i], :] = out[strips[i], :] + sign * add
        if m == count:
            continue
        sums = table[m]
        for part in ends + strips:
            v = img[m, part, :]
            others = [img[q, part, :] for q in range(m)] + [v, res_ref[part, :]]
            if part in strips:
                v = jnp.where(mid_a, v, 0.0)
            sums = [acc + total(v * o) for acc, o in zip(sums, others)]
        pair = jnp.logical_or(lane8 == 16 * sub8 + m, lane8 == 16 * m + sub8)
        packed = packed + jnp.where(jnp.logical_and(pair, sub8 <= m), column(sums[: m + 1]), 0.0)
        starts.append(sums[m + 1])
    packed = packed + jnp.where(lane8 == 16 * sub8 + count, column(starts), 0.0)

    far_first = sorted(
        [(i, j) for i in range(gxn) for j in range(gyn) if i or j],
        key=lambda t: (abs(t[1] - gyn // 2), abs(t[0] - gxn // 2)),
    )

    def all_sum(k, row):
        psend[k] = row
        slots[k, me] = row

        def send(gi, gj):
            pltpu.make_async_remote_copy(
                src_ref=psend.at[k], dst_ref=slots.at[k, me],
                send_sem=ps_sem.at[k], recv_sem=pr_sem.at[k], **at_dev(gi, gj),
            ).start()

        if n <= 64:
            for i, j in far_first:
                send(gis[i], gjs[j])
        else:
            def step(t, _):
                peer = lax.rem(me + t, n)
                send(peer // gyn, lax.rem(peer, gyn))
                return 0

            lax.fori_loop(1, n, step, 0)
        most = slots.at[k, pl.ds(0, n - 1)]
        pltpu.make_async_copy(most, most, pr_sem.at[k]).wait()
        out = jnp.sum(slots[k], axis=0)
        return out

    row = all_sum(0, jnp.sum(packed, axis=0, keepdims=True))

    wrow = jnp.broadcast_to(row, (8, lanes))
    mat = zero8
    for m in range(count):
        moved = wrow if m == 0 else pltpu.roll(wrow, lanes - 16 * m, 1)
        mat = jnp.where(sub8 == m, moved, mat)
    mat = jnp.where(lane8 <= count, mat, 0.0) + jnp.where(lane8 == 16 + sub8, 1.0, 0.0)
    for k in range(count):
        pivot = mat[k : k + 1, :] / mat[k : k + 1, k : k + 1]
        mat = jnp.where(sub8 == k, pivot, mat - mat[:, k : k + 1] * pivot)
    inverse = pltpu.roll(mat, lanes - 16, 1)

    def whole(v):
        return jnp.concatenate([jnp.broadcast_to(v, (8, lanes))] * (b // 8), axis=0)

    coeffs = [whole(mat[m : m + 1, count : count + 1]) for m in range(count)]

    for x in range(a):
        rows = slice(x * b, x * b + b)
        res = res_ref[rows, :]
        for m in range(count):
            res = res - coeffs[m] * img[m, rows, :]
        rwide[0, pl.ds(base(x), b), :] = res

    def first_solution(x):
        rows = slice(x * b, x * b + b)
        sol = fg_ref[rows, :]
        for m in range(count):
            sol = sol + coeffs[m] * rec_ref[m, rows, :].astype(F32)
        sol_ref[rows, :] = sol

    later = first_solution

    bits = ((0, 0), (0, 1), (1, 0))

    for outer in range(OUTER):
        w = rwide.at[outer]
        for i in range(GHOST):
            ysend[outer, 0, i] = w[pl.ds(base(0) + i, a, stride=S), :]
            ysend[outer, 1, i] = w[pl.ds(base(0) + b - 1 - i, a, stride=S), :]
        for s in range(4, 8):
            for i, (p, q) in enumerate(bits):
                x = p if steps[s][0] < 0 else a - 1 - p
                y = q if steps[s][1] < 0 else b - 1 - q
                csend[outer, s - 4, i] = w[pl.ds(base(x) + y, 1), :]
        each((4, 5, 6, 7, 2, 3, 0, 1), lambda s: all_do(deep_copies(outer, s), "start"))
        for x in range(a):
            later(x)

        accs = [zero8] * count
        for x in range(a):
            rows = slice(x * b, x * b + b)
            res = w[pl.ds(base(x), b), :]
            accs = [acc + total(img[m, rows, :] * res) for m, acc in enumerate(accs)]
        alongs = column(accs)
        each(range(8), lambda s: all_do(deep_copies(outer, opposite[s]), "wait_recv"))
        for i in range(GHOST):
            w[pl.ds(base(0) - 1 - i, a, stride=S), :] = yrecv[outer, 0, i]
            w[pl.ds(base(0) + b + i, a, stride=S), :] = yrecv[outer, 1, i]
        for s in range(4, 8):
            for i, (p, q) in enumerate(bits):
                x = -1 - p if steps[s][0] < 0 else a + p
                y = -1 - q if steps[s][1] < 0 else b + q
                w[pl.ds(base(x) + y, 1), :] = crecv[outer, s - 4, i]
        for x in range(-GHOST, a + GHOST):
            uwide[0, span(x), :] = fwide[span(x), :] * (w[span(x), :] * (1.0 / CENTER))
        rho = 1.0 / SIGMA
        for sweep in range(SWEEPS):
            rho_new = 1.0 / (2.0 * SIGMA - rho)
            grow = SWEEPS - 1 - sweep
            for x in range(-grow, a + grow):
                at, size = (base(x), b) if grow == 0 else (S * (x + GHOST), S)
                rows = pl.ds(at, size)
                f = fwide[rows, :]
                old = w[rows, :] if sweep == 0 else rem[rows, :]
                d = old * (1.0 / CENTER) if sweep == 0 else dwide[rows, :]
                left = old - (diag[rows, :] * d - f * near(uwide.at[sweep], at, size))
                cbuf[rows, :] = d if sweep == 0 else cbuf[rows, :] + d
                rem[rows, :] = left
                if sweep + 1 < SWEEPS:
                    d = (rho_new * rho) * d + (2.0 * rho_new / HALF) * left
                    dwide[rows, :] = d
                    uwide[sweep + 1, rows, :] = f * d
            rho = rho_new

        accs = [zero8] * (count + 2)
        for x in range(a):
            rows = slice(x * b, x * b + b)
            at = pl.ds(base(x), b)
            res = rwide[outer, at, :]
            image = res - rem[at, :]
            others = [img[m, rows, :] for m in range(count)] + [res, image]
            accs = [acc + total(image * o) for acc, o in zip(accs, others)]
        packed = (
            jnp.where(lane8 == sub8, column(accs[:count]), 0.0)
            + jnp.where(lane8 == sub8 + 8, alongs, 0.0)
            + jnp.where(lane8 == sub8 + 16, column(accs[count:]), 0.0)
        )
        row = all_sum(1 + outer, jnp.sum(packed, axis=0, keepdims=True))
        onto = jnp.sum(jnp.where(lane8 == sub8, jnp.broadcast_to(row, (8, lanes)), 0.0), axis=1, keepdims=True)
        y = jnp.sum(onto * inverse, axis=0, keepdims=True)
        y = jnp.where(row1 < count, y, 0.0)
        along = pltpu.roll(jnp.broadcast_to(row, (8, lanes)), lanes - 8, 1)[0:1]
        numerator = row[:, 16:17] - jnp.sum(y * along, axis=1, keepdims=True)
        denominator = row[:, 17:18] - jnp.sum(y * row, axis=1, keepdims=True)
        step = whole(numerator / denominator)
        ys = [whole(y[:, m : m + 1]) for m in range(count)]

        for x in range(a):
            rows = slice(x * b, x * b + b)
            at = pl.ds(base(x), b)
            res = rwide[outer, at, :]
            image = res - rem[at, :]
            for m in range(count):
                image = image - ys[m] * img[m, rows, :]
            res = res - step * image
            if outer + 1 < OUTER:
                rwide[outer + 1, at, :] = res
            else:
                res_ref[rows, :] = res

        def solution_update(x, step=step, ys=ys):
            rows = slice(x * b, x * b + b)
            c = cbuf[pl.ds(base(x), b), :]
            for m in range(count):
                c = c - ys[m] * rec_ref[m, rows, :].astype(F32)
            sol_ref[rows, :] = sol_ref[rows, :] + step * c

        later = solution_update

    for x in range(a):
        later(x)

    for k in range(OUTER + 1):
        most = slots.at[k, pl.ds(0, n - 1)]
        pltpu.make_async_copy(most, most, ps_sem.at[k]).wait()
    each(range(8), lambda s: ground_copy(s).wait_send())
    for m in range(nf):
        each(range(4), lambda s: field_copy(m, s).wait_send())
    for r in range(OUTER):
        each(range(8), lambda s: all_do(deep_copies(r, s), "wait_send"))


def store(sol_ref, res_ref, sol_out, res_out, sem):
    cps = [
        pltpu.make_async_copy(sol_ref, sol_out, sem.at[0]),
        pltpu.make_async_copy(res_ref, res_out, sem.at[1]),
    ]
    for cp in cps:
        cp.start()
    for cp in cps:
        cp.wait()


def solution(mesh):
    gxn, gyn = mesh.shape["gx"], mesh.shape["gy"]

    def local(right_side, first_guess, recycled, heights, ground_codes):
        a, b, nz = right_side.shape
        count = recycled.shape[0]
        field = jax.ShapeDtypeStruct((a * b, nz), F32)
        vm = pl.BlockSpec(memory_space=pltpu.VMEM)
        wide_f = pltpu.VMEM(((a + 2 * GHOST) * (b + 16), nz), F32)
        n = gxn * gyn
        hbm = pl.BlockSpec(memory_space=pltpu.HBM)
        dma = pltpu.SemaphoreType.DMA
        sol, res = pl.pallas_call(
            functools.partial(kernel, gxn, gyn, count, a, b),
            out_shape=(field, field),
            in_specs=[hbm] * 5,
            out_specs=(vm, vm),
            scratch_shapes=[
                pltpu.VMEM((a * b, nz), F32),
                pltpu.VMEM((a * b, nz), F32),
                pltpu.VMEM((count, a * b, nz), jnp.bfloat16),
                pltpu.VMEM((2, a, b), jnp.int32),
                pltpu.VMEM((8, 2, a, b), jnp.int32),
                pltpu.VMEM((count + 1, (a + 2) * (b + 16), nz), F32),
                pltpu.VMEM((count + 1, 2, b, nz), F32),
                pltpu.VMEM((count + 1, 2, a, nz), F32),
                pltpu.VMEM((count + 1, 2, a, nz), F32),
                pltpu.VMEM((OUTER,) + wide_f.shape, F32),
                pltpu.VMEM((OUTER, 2, GHOST, a, nz), F32),
                pltpu.VMEM((OUTER, 2, GHOST, a, nz), F32),
                pltpu.VMEM((OUTER, 4, 3, 1, nz), F32),
                pltpu.VMEM((OUTER, 4, 3, 1, nz), F32),
                wide_f,
                wide_f,
                pltpu.VMEM((SWEEPS,) + wide_f.shape, F32),
                wide_f,
                wide_f,
                wide_f,
                pltpu.VMEM((count, a * b, nz), F32),
                pltpu.VMEM((OUTER + 1, 1, nz), F32),
                pltpu.VMEM((OUTER + 1, n, 1, nz), F32),
                dma((4 + count,)),
                dma((8,)),
                dma((8,)),
                dma((count + 1, 4)),
                dma((count + 1, 4)),
                dma((OUTER, 8, GHOST)),
                dma((OUTER, 8, GHOST)),
                dma((OUTER + 1,)),
                dma((OUTER + 1,)),
                pltpu.SemaphoreType.REGULAR((max(gyn.bit_length(), 1), 2)),
            ],
            compiler_params=pltpu.CompilerParams(
                collective_id=0, has_side_effects=True, vmem_limit_bytes=32 * 2**20
            ),
        )(*[
            pltpu.with_memory_space_constraint(v, pltpu.HBM)
            for v in (
                right_side.reshape(a * b, nz),
                first_guess.reshape(a * b, nz),
                recycled.reshape(count, a * b, nz),
                heights,
                ground_codes,
            )
        ])
        sol, res = pl.pallas_call(
            store,
            out_shape=(field, field),
            in_specs=[vm] * 2,
            out_specs=(hbm, hbm),
            scratch_shapes=[dma((2,))],
            compiler_params=pltpu.CompilerParams(vmem_limit_bytes=4 * 2**20),
        )(sol, res)
        return sol.reshape(a, b, nz), res.reshape(a, b, nz)

    placed = (
        P("gx", "gy", None),
        P("gx", "gy", None),
        P(None, "gx", "gy", None),
        P("gx", "gy"),
        P("gx", "gy"),
    )
    return jax.shard_map(
        local,
        mesh=mesh,
        in_specs=placed,
        out_specs=(P("gx", "gy", None), P("gx", "gy", None)),
        check_vma=False,
    )
```

```python
import functools

import jax
import jax.numpy as jnp
from jax import lax
from jax.experimental import pallas as pl
from jax.experimental.pallas import tpu as pltpu
from jax.sharding import PartitionSpec as P

OUTER = 2
SWEEPS = 3
GHOST = SWEEPS
NEAR = 2

CENTER = 7.25
HALF = 6.75
SIGMA = 7.25 / 6.75

F32 = jnp.float32


def kernel(
    gxn, gyn, count, a, b,
    rs_hbm, fg_hbm, rec_hbm, h_hbm, code_hbm,
    sol_ref, res_ref,
    rs_ref, fg_ref, rec_ref, ground, near_ground,
    wide0, xrecv0, ysend0, yrecv0, rwide, ysend, yrecv, csend, crecv,
    fwide, diag, uwide, dwide, rem, cbuf, img, psend, slots,
    wown, wysend, wcsend, wxrecv, wyrecv, wcrecv, iysend, icsend, ixrecv, iyrecv, icrecv,
    in_sem, gs_sem, gr_sem, hs_sem, hr_sem, ds_sem, dr_sem, ps_sem, pr_sem, ws_sem, wr_sem, is_sem, ir_sem, known,
):
    lanes = 128
    S = b + 16
    n = gxn * gyn
    nf = count + 1
    gx = lax.axis_index("gx")
    gy = lax.axis_index("gy")
    me = gx * gyn + gy

    def at_dev(i, j):
        return dict(device_id={"gx": i, "gy": j}, device_id_type=pl.DeviceIdType.MESH)

    loads = [
        pltpu.make_async_copy(h_hbm, ground.at[0], in_sem.at[0]),
        pltpu.make_async_copy(code_hbm, ground.at[1], in_sem.at[1]),
        pltpu.make_async_copy(fg_hbm, fg_ref, in_sem.at[2]),
        pltpu.make_async_copy(rs_hbm, rs_ref, in_sem.at[3]),
    ] + [pltpu.make_async_copy(rec_hbm.at[m], rec_ref.at[m], in_sem.at[4 + m]) for m in range(count)]
    for cp in loads:
        cp.start()

    barrier = pltpu.get_barrier_semaphore()

    gis = [lax.rem(gx + i, gxn) for i in range(gxn)]
    gjs = [lax.rem(gy + j, gyn) for j in range(gyn)]

    greeters = -1
    for j in sorted(range(-NEAR, NEAR + 1), key=abs):
        inside = jnp.logical_and(gy + j >= 0, gy + j < gyn)
        greeters = greeters + jnp.where(inside, gxn, 0)

        @pl.when(inside)
        def _(j=j):
            for i in range(gxn):
                if i or j:
                    pl.semaphore_signal(barrier, inc=1, **at_dev(gis[i], gy + j))

    stages, reach = [], NEAR
    while reach < gyn - 1:
        stages.append(reach)
        reach *= 2

    def stage(k, act):
        for side, j in enumerate((-stages[k], stages[k])):
            @pl.when(jnp.logical_and(gy + j >= 0, gy + j < gyn))
            def _(side=side, j=j):
                if act == "signal":
                    pl.semaphore_signal(known.at[k, 1 - side], inc=1, **at_dev(gx, gy + j))
                else:
                    pl.semaphore_wait(known.at[k, side], 1)

    def base0(x):
        return S * (x + 1) + 8

    def base(x):
        return S * (x + GHOST) + 8

    def span(x):
        return pl.ds(S * (x + GHOST), S)

    lane8 = lax.broadcasted_iota(jnp.int32, (8, lanes), 1)
    sub8 = lax.broadcasted_iota(jnp.int32, (8, lanes), 0)
    row1 = lax.broadcasted_iota(jnp.int32, (1, lanes), 1)

    steps = ((-1, 0), (1, 0), (0, -1), (0, 1), (-1, -1), (-1, 1), (1, -1), (1, 1))
    opposite = [steps.index((-i, -j)) for i, j in steps]
    have, peers = [], []
    for i, j in steps:
        ok = None
        for at, size, by in ((gx, gxn, i), (gy, gyn, j)):
            if by:
                one = at > 0 if by < 0 else at < size - 1
                ok = one if ok is None else jnp.logical_and(ok, one)
        have.append(ok)
        peers.append(at_dev(gx + i, gy + j))

    def ground_copy(s):
        return pltpu.make_async_remote_copy(
            src_ref=ground, dst_ref=near_ground.at[opposite[s]],
            send_sem=gs_sem.at[s], recv_sem=gr_sem.at[opposite[s]], **peers[s],
        )

    def field_copy(m, s):
        w = wide0.at[m]
        src = (
            w.at[pl.ds(base0(0), b), :], w.at[pl.ds(base0(a - 1), b), :],
            ysend0.at[m, 0], ysend0.at[m, 1],
        )[s]
        dst = (
            xrecv0.at[m, 1], xrecv0.at[m, 0],
            yrecv0.at[m, 1], yrecv0.at[m, 0],
        )[s]
        return pltpu.make_async_remote_copy(
            src_ref=src, dst_ref=dst,
            send_sem=hs_sem.at[m, s], recv_sem=hr_sem.at[m, opposite[s]], **peers[s],
        )

    def send_to(s, src, dst, sends, recvs):
        return pltpu.make_async_remote_copy(
            src_ref=src, dst_ref=dst, send_sem=sends, recv_sem=recvs, **peers[s]
        )

    def deep_copies(s):
        w = rwide.at[0]
        if s < 2:
            pieces = [
                (
                    w.at[pl.ds(base(i if s == 0 else a - GHOST + i), b), :],
                    w.at[pl.ds(base(a + i if s == 0 else i - GHOST), b), :],
                )
                for i in range(GHOST)
            ]
        elif s < 4:
            pieces = [(ysend.at[s - 2], yrecv.at[3 - s])]
        else:
            pieces = [(csend.at[s - 4], crecv.at[opposite[s] - 4])]
        return [
            send_to(s, p, q, ds_sem.at[s, i], dr_sem.at[opposite[s], i])
            for i, (p, q) in enumerate(pieces)
        ]

    def face(field, s):
        return field.at[pl.ds(0 if s == 0 else (a - GHOST) * b, GHOST * b), :]

    def w_copy(s):
        if s < 2:
            src, dst = face(wown.at[0], s), wxrecv.at[1 - s]
        elif s < 4:
            src, dst = wysend.at[s - 2], wyrecv.at[3 - s]
        else:
            src, dst = wcsend.at[s - 4], wcrecv.at[opposite[s] - 4]
        return send_to(s, src, dst, ws_sem.at[s], wr_sem.at[opposite[s]])

    def image_copy(m, s):
        if s < 2:
            src, dst = face(img.at[m], s), ixrecv.at[m, 1 - s]
        elif s < 4:
            src, dst = iysend.at[m, s - 2], iyrecv.at[m, 3 - s]
        else:
            src, dst = icsend.at[s - 4], icrecv.at[opposite[s] - 4]
        return send_to(s, src, dst, is_sem.at[m, s], ir_sem.at[m, opposite[s]])

    def each(sides, act):
        for s in sides:
            @pl.when(have[s])
            def _(s=s):
                act(s)

    def all_do(cps, what):
        for cp in cps:
            getattr(cp, what)()

    zeros = jnp.zeros((b, lanes), F32)
    ones = jnp.ones((b, lanes), jnp.bfloat16)
    yi = lax.broadcasted_iota(jnp.int32, (S, b), 0)
    ji = lax.broadcasted_iota(jnp.int32, (S, b), 1)
    lane_f = lax.broadcasted_iota(jnp.int32, (S, lanes), 1).astype(F32)
    lane_s = lax.broadcasted_iota(jnp.int32, (S, lanes), 1)

    def spread(tables, i):
        left, mid, right = [jnp.broadcast_to(t[i : i + 1, :].astype(F32), (S, b)) for t in tables]
        pick = jnp.where(yi - 8 == ji, mid, 0.0)
        pick = jnp.where(yi == ji - (b - 8), left, pick)
        pick = jnp.where(yi - (b + 8) == ji, right, pick)
        return jnp.dot(pick.astype(jnp.bfloat16), ones, preferred_element_type=F32)

    def mask_row(x, trio, i):
        high = spread([t.at[0] for t in trio], i)
        code = spread([t.at[1] for t in trio], i)
        fwide[span(x), :] = jnp.where(lane_f >= high, 1.0, 0.0)
        bottom = jnp.where(code == 1.0, 0.5, 0.0) + jnp.where(code == 2.0, 2.0, 0.0)
        diag[span(x), :] = jnp.where(lane_s == 0, bottom, 0.0) + jnp.where(
            lane_s == lanes - 1, 1.0, 0.0
        )

    def fluid(x):
        return fwide[pl.ds(base(x), b), :]

    own_y = jnp.logical_and(lax.broadcasted_iota(jnp.int32, (S, lanes), 0) >= 8,
                            lax.broadcasted_iota(jnp.int32, (S, lanes), 0) < b + 8)

    def near(w, at, size):
        c = w[pl.ds(at, size), :]
        lane = lax.broadcasted_iota(jnp.int32, (size, lanes), 1)
        up = jnp.where(lane == lanes - 1, 0.0, pltpu.roll(c, lanes - 1, 1))
        down = jnp.where(lane == 0, 0.0, pltpu.roll(c, 1, 1))
        return (
            (w[pl.ds(at + S, size), :] + w[pl.ds(at - S, size), :])
            + (w[pl.ds(at + 1, size), :] + w[pl.ds(at - 1, size), :])
            + (up + down)
        )

    all_do(loads[:2], "wait")
    for x in (-1, a):
        fwide[span(x), :] = jnp.zeros((S, lanes), F32)
    for x in range(a):
        mask_row(x, (ground,) * 3, x)
        fwide[span(x), :] = jnp.where(own_y, fwide[span(x), :], 0.0)

    def set_diag(x):
        f = fwide[span(x), :]
        diag[span(x), :] = f * (near(fwide, S * (x + GHOST), S) + diag[span(x), :]) + (1.0 - f)

    def prepare(m):
        loads[2 if m == count else 4 + m].wait()
        w = wide0.at[m]
        for x in range(a):
            rows = slice(x * b, x * b + b)
            v = fg_ref[rows, :] if m == count else rec_ref[m, rows, :].astype(F32)
            w[pl.ds(base0(x), b), :] = fluid(x) * v
        ysend0[m, 0] = w[pl.ds(S + 8, a, stride=S), :]
        ysend0[m, 1] = w[pl.ds(S + 8 + b - 1, a, stride=S), :]

    order = [count] + list(range(count))
    early = order[: (nf + 1) // 2]
    for m in early:
        prepare(m)
    pl.semaphore_wait(barrier, greeters)
    each((4, 5, 6, 7, 2, 3, 0, 1), lambda s: ground_copy(s).start())
    for m in early:
        each((2, 3, 0, 1), lambda s: field_copy(m, s).start())
    for k in range(len(stages)):
        if k == 0:
            stage(k, "signal")
    for m in order[len(early) :]:
        prepare(m)
        each((2, 3, 0, 1), lambda s: field_copy(m, s).start())

    zeros_a = jnp.zeros((a, lanes), F32)
    for s in range(8):
        @pl.when(jnp.logical_not(have[s]))
        def _(s=s):
            near_ground[s, 0] = jnp.full((a, b), 255, jnp.int32)
            near_ground[s, 1] = jnp.zeros((a, b), jnp.int32)
            if s < 2:
                wxrecv[s] = jnp.zeros((GHOST * b, lanes), F32)
                for m in range(nf):
                    xrecv0[m, s] = zeros
                for m in range(count):
                    ixrecv[m, s] = jnp.zeros((GHOST * b, lanes), F32)
                for i in range(GHOST):
                    rwide[0, pl.ds(base(i - GHOST if s == 0 else a + i), b), :] = zeros
            elif s < 4:
                wyrecv[s - 2] = jnp.zeros((GHOST * a, lanes), F32)
                for m in range(nf):
                    yrecv0[m, s - 2] = zeros_a
                for m in range(count):
                    iyrecv[m, s - 2] = jnp.zeros((GHOST * a, lanes), F32)
                for i in range(GHOST):
                    yrecv[s - 2, i] = zeros_a
            else:
                crecv[s - 4] = jnp.zeros((8, lanes), F32)
                wcrecv[s - 4] = jnp.zeros((8, lanes), F32)
                icrecv[s - 4] = jnp.zeros((count * GHOST, lanes), F32)

    for m in range(nf):
        w = wide0.at[m]
        for x in (-1, a):
            w[pl.ds(base0(x), b), :] = zeros
        for y in (-1, b):
            w[pl.ds(base0(0) + y, a, stride=S), :] = zeros_a
    for x in range(a):
        set_diag(x)

    zero8 = jnp.zeros((8, lanes), F32)

    def tiles(v):
        return [v[i : i + 8] for i in range(0, v.shape[0], 8)]

    def total(v):
        return functools.reduce(jnp.add, tiles(v))

    table = {}
    loads[3].wait()
    waited = 0
    for turn, m in enumerate(order):
        sums = [zero8] * (m + 2)
        for x in range(a):
            rows = slice(x * b, x * b + b)
            dg = diag[pl.ds(base(x), b), :]
            flow = fluid(x) * near(wide0.at[m], base0(x), b)
            if m == count:
                res_ref[rows, :] = rs_ref[rows, :] - (dg * fg_ref[rows, :] - flow)
                continue
            v = dg * rec_ref[m, rows, :].astype(F32) - flow
            img[m, rows, :] = v
            if 0 < x < a - 1:
                inner = tiles(v)
                inner[0] = jnp.where(sub8 > 0, inner[0], 0.0)
                inner[-1] = jnp.where(sub8 < 7, inner[-1], 0.0)
                others = [img[q, rows, :] for q in range(m)] + [v, res_ref[rows, :]]
                sums = [
                    acc + functools.reduce(jnp.add, [i * j for i, j in zip(inner, tiles(o))])
                    for acc, o in zip(sums, others)
                ]
        if m < count:
            table[m] = sums
        if turn in (2, 6) and waited < len(stages):
            stage(waited, "wait")
            waited += 1
            if waited < len(stages):
                stage(waited, "signal")
    while waited < len(stages):
        stage(waited, "wait")
        waited += 1
        if waited < len(stages):
            stage(waited, "signal")

    each(range(8), lambda s: ground_copy(opposite[s]).wait_recv())
    for x in range(-GHOST, a + GHOST):
        if x < 0:
            trio, i = (near_ground.at[4], near_ground.at[0], near_ground.at[5]), a + x
        elif x < a:
            trio, i = (near_ground.at[2], ground, near_ground.at[3]), x
        else:
            trio, i = (near_ground.at[6], near_ground.at[1], near_ground.at[7]), x - a
        mask_row(x, trio, i)

    for x in range(1 - GHOST, a + GHOST - 1):
        set_diag(x)

    def column(items):
        rows = [jnp.sum(v, axis=0, keepdims=True) for v in items]
        if len(rows) < 8:
            rows.append(jnp.zeros((8 - len(rows), lanes), F32))
        return jnp.sum(jnp.concatenate(rows, axis=0), axis=1, keepdims=True)

    bits = ((0, 0), (0, 1), (1, 0))

    def corner_at(s, p, q):
        return p if steps[s][0] < 0 else a - 1 - p, q if steps[s][1] < 0 else b - 1 - q

    def take_strips(field, out):
        for i in range(GHOST):
            for side, y in enumerate((i, b - 1 - i)):
                out[side, i * a : (i + 1) * a, :] = field[pl.ds(y, a, stride=b), :]

    def image_strips(fields):
        for m in fields:
            take_strips(img.at[m], iysend.at[m])

    def share(fields):
        for m in fields:
            each((2, 3, 0, 1), lambda s: image_copy(m, s).start())

    first, second = count // 4, count * 3 // 4

    sub_a = lax.broadcasted_iota(jnp.int32, (a, lanes), 0)
    mid_a = jnp.logical_and(sub_a > 0, sub_a < a - 1)
    ends = [slice(x * b, x * b + b) for x in (0, a - 1)]
    strips = [pl.ds(y, a, stride=b) for y in (0, b - 1)]
    packed = zero8
    starts = []
    for m in order:
        each(range(4), lambda s: field_copy(m, opposite[s]).wait_recv())
        out = res_ref if m == count else img.at[m]
        sign = -1.0 if m == count else 1.0
        for i, (x, g) in enumerate(((0, -1), (a - 1, a))):
            add = fluid(g) * wide0[m, pl.ds(base0(x), b), :] - fluid(x) * xrecv0[m, i]
            out[ends[i], :] = out[ends[i], :] + sign * add
        for i, (y, g) in enumerate(((0, -1), (b - 1, b))):
            f_out = fwide[pl.ds(base(0) + g, a, stride=S), :]
            f_own = fwide[pl.ds(base(0) + y, a, stride=S), :]
            add = f_out * ysend0[m, i] - f_own * yrecv0[m, i]
            out[strips[i], :] = out[strips[i], :] + sign * add
        if m == count:
            continue
        sums = table[m]
        for part in ends + strips:
            v = img[m, part, :]
            others = [img[q, part, :] for q in range(m)] + [v, res_ref[part, :]]
            if part in strips:
                v = jnp.where(mid_a, v, 0.0)
            sums = [acc + total(v * o) for acc, o in zip(sums, others)]
        pair = jnp.logical_or(lane8 == 16 * sub8 + m, lane8 == 16 * m + sub8)
        packed = packed + jnp.where(jnp.logical_and(pair, sub8 <= m), column(sums[: m + 1]), 0.0)
        starts.append(sums[m + 1])
        if m < first:
            image_strips([m])
            share([m])
    packed = packed + jnp.where(lane8 == 16 * sub8 + count, column(starts), 0.0)

    far_first = sorted(
        [(i, j) for i in range(gxn) for j in range(gyn) if i or j],
        key=lambda t: (abs(t[1] - gyn // 2), abs(t[0] - gxn // 2)),
    )

    def sum_start(k, row):
        psend[k] = row
        slots[k, me] = row

        def send(gi, gj):
            pltpu.make_async_remote_copy(
                src_ref=psend.at[k], dst_ref=slots.at[k, me],
                send_sem=ps_sem.at[k], recv_sem=pr_sem.at[k], **at_dev(gi, gj),
            ).start()

        if n <= 64:
            for i, j in far_first:
                send(gis[i], gjs[j])
        else:
            def step(t, _):
                peer = lax.rem(me + t, n)
                send(peer // gyn, lax.rem(peer, gyn))
                return 0

            lax.fori_loop(1, n, step, 0)
    def sum_done(k):
        most = slots.at[k, pl.ds(0, n - 1)]
        pltpu.make_async_copy(most, most, pr_sem.at[k]).wait()
        return jnp.sum(slots[k], axis=0)

    def widened(v, size):
        return jnp.broadcast_to(v, (size, lanes))

    sum_start(0, jnp.sum(packed, axis=0, keepdims=True))
    image_strips(range(first, second))
    share(range(first, second))
    for s in range(4, 8):
        for i, (p, q) in enumerate(bits):
            x, y = corner_at(s, p, q)
            for m in range(count):
                icsend[s - 4, pl.ds(GHOST * m + i, 1), :] = img[m, pl.ds(x * b + y, 1), :]
    each(range(4, 8), lambda s: image_copy(0, s).start())
    image_strips(range(second, count))
    for s in range(4):
        csend[s] = zero8
        wcsend[s] = zero8
    row = sum_done(0)

    wrow = jnp.broadcast_to(row, (8, lanes))
    gram = zero8
    for m in range(count):
        moved = wrow if m == 0 else pltpu.roll(wrow, lanes - 16 * m, 1)
        gram = jnp.where(sub8 == m, moved, gram)
    cols = [jnp.broadcast_to(gram[:, k : k + 1], (8, lanes)) for k in range(count + 1)]
    start = cols[count]
    cols += [jnp.where(sub8 == k, 1.0, 0.0) for k in range(count)]
    for k in range(count):
        this = cols[k]
        scale = 1.0 / widened(this[k : k + 1], 8)
        for j in list(range(k + 1, count + 1)) + list(range(count + 1, count + 2 + k)):
            pivot = widened(cols[j][k : k + 1], 8) * scale
            cols[j] = jnp.where(sub8 == k, pivot, cols[j] - this * pivot)
    coef = cols[count]
    coeffs = [coef[m : m + 1] for m in range(count)]

    for x in range(a):
        rows = slice(x * b, x * b + b)
        res = res_ref[rows, :]
        for m in range(count):
            res = res - widened(coeffs[m], b) * img[m, rows, :]
        rwide[0, pl.ds(base(x), b), :] = res

    w = rwide.at[0]
    for i in range(GHOST):
        ysend[0, i] = w[pl.ds(base(0) + i, a, stride=S), :]
        ysend[1, i] = w[pl.ds(base(0) + b - 1 - i, a, stride=S), :]
    for s in range(4, 8):
        for i, (p, q) in enumerate(bits):
            x, y = corner_at(s, p, q)
            csend[s - 4, pl.ds(i, 1), :] = w[pl.ds(base(x) + y, 1), :]
    each((4, 5, 6, 7, 2, 3, 0, 1), lambda s: all_do(deep_copies(s), "start"))

    inverse = zero8
    for k in range(count):
        inverse = jnp.where(lane8 == k, cols[count + 1 + k], inverse)
    gram = jnp.where(lane8 < count, gram, 0.0)

    def times(matrix, row):
        return jnp.sum(matrix * row, axis=1, keepdims=True)

    def as_row(col):
        return jnp.sum(jnp.where(lane8 == sub8, col, 0.0), axis=0, keepdims=True)

    along = start - times(gram, as_row(coef))

    for x in range(a):
        rows = slice(x * b, x * b + b)
        sol = fg_ref[rows, :]
        for m in range(count):
            sol = sol + widened(coeffs[m], b) * rec_ref[m, rows, :].astype(F32)
        sol_ref[rows, :] = sol

    each((2, 3), lambda s: all_do(deep_copies(s), "wait_send"))
    share(range(second, count))
    each(range(8), lambda s: all_do(deep_copies(opposite[s]), "wait_recv"))

    def put_strip(w, side, i, v):
        y = -1 - i if side == 0 else b + i
        w[pl.ds(base(0) + y, a, stride=S), :] = v

    def put_corner(w, s, v):
        for i, (p, q) in enumerate(bits):
            x = -1 - p if steps[s][0] < 0 else a + p
            y = -1 - q if steps[s][1] < 0 else b + q
            w[pl.ds(base(x) + y, 1), :] = v[i : i + 1]

    for i in range(GHOST):
        for side in range(2):
            put_strip(w, side, i, yrecv[side, i])
    for s in range(4, 8):
        put_corner(w, s, crecv[s - 4])

    for outer in range(OUTER):
        last = outer + 1 == OUTER
        w = rwide.at[outer]
        for x in range(-GHOST, a + GHOST):
            uwide[0, span(x), :] = fwide[span(x), :] * (w[span(x), :] * (1.0 / CENTER))
        rho = 1.0 / SIGMA
        for sweep in range(SWEEPS):
            rho_new = 1.0 / (2.0 * SIGMA - rho)
            grow = SWEEPS - 1 - sweep
            for x in range(-grow, a + grow):
                at, size = (base(x), b) if grow == 0 else (S * (x + GHOST), S)
                rows = pl.ds(at, size)
                f = fwide[rows, :]
                old = w[rows, :] if sweep == 0 else rem[rows, :]
                d = old * (1.0 / CENTER) if sweep == 0 else dwide[rows, :]
                left = old - (diag[rows, :] * d - f * near(uwide.at[sweep], at, size))
                if 0 <= x < a:
                    own = slice(x * b, x * b + b)
                    mine = d if grow == 0 else d[8 : 8 + b]
                    cbuf[outer, own, :] = mine if sweep == 0 else cbuf[outer, own, :] + mine
                rem[rows, :] = left
                if sweep + 1 < SWEEPS:
                    d = (rho_new * rho) * d + (2.0 * rho_new / HALF) * left
                    dwide[rows, :] = d
                    uwide[sweep + 1, rows, :] = f * d
            rho = rho_new

        accs = [zero8] * (count + 2)
        for x in range(a):
            rows = slice(x * b, x * b + b)
            at = pl.ds(base(x), b)
            res = w[at, :]
            image = res - rem[at, :]
            wown[outer, rows, :] = image
            others = [img[m, rows, :] for m in range(count)] + [res, image]
            accs = [acc + total(image * o) for acc, o in zip(accs, others)]
        packed = (
            jnp.where(lane8 == sub8, column(accs[:count]), 0.0)
            + jnp.where(lane8 == sub8 + 16, column(accs[count:]), 0.0)
        )
        sum_start(1 + outer, jnp.sum(packed, axis=0, keepdims=True))
        if not last:
            take_strips(wown.at[outer], wysend)
            for s in range(4, 8):
                for i, (p, q) in enumerate(bits):
                    x, y = corner_at(s, p, q)
                    wcsend[s - 4, pl.ds(i, 1), :] = wown[outer, pl.ds(x * b + y, 1), :]
            each((4, 5, 6, 7, 2, 3, 0, 1), lambda s: w_copy(s).start())
        else:
            for x in range(a):
                earlier(x)
        row = sum_done(1 + outer)

        onto_row = jnp.where(lane8 < count, jnp.broadcast_to(row, (8, lanes)), 0.0)
        y = times(inverse, onto_row)
        onto = jnp.sum(jnp.where(lane8 == sub8, onto_row, 0.0), axis=1, keepdims=True)
        numerator = row[:, 16:17] - jnp.sum(y * along, axis=0, keepdims=True)[:, 0:1]
        denominator = row[:, 17:18] - jnp.sum(y * onto, axis=0, keepdims=True)
        step = jnp.broadcast_to(numerator / denominator, (1, lanes))
        y = jnp.broadcast_to(y, (8, lanes))
        ys = [y[m : m + 1] for m in range(count)]

        def stepped(res, image, parts):
            size = res.shape[0]
            for m in range(count):
                image = image - widened(ys[m], size) * parts(m)
            return res - widened(step, size) * image

        for x in range(a):
            rows = slice(x * b, x * b + b)
            at = pl.ds(base(x), b)
            res = stepped(w[at, :], wown[outer, rows, :], lambda m: img[m, rows, :])
            if last:
                res_ref[rows, :] = res
            else:
                rwide[outer + 1, at, :] = res

        def solution_update(x, outer=outer, step=step, ys=ys):
            rows = slice(x * b, x * b + b)
            c = cbuf[outer, rows, :]
            for m in range(count):
                c = c - widened(ys[m], b) * rec_ref[m, rows, :].astype(F32)
            sol_ref[rows, :] = sol_ref[rows, :] + widened(step, b) * c

        if last:
            for x in range(a):
                solution_update(x)
            continue
        earlier = solution_update

        for m in range(count):
            each(range(4), lambda s: image_copy(m, opposite[s]).wait_recv())
        each(range(4, 8), lambda s: image_copy(0, opposite[s]).wait_recv())
        each(range(8), lambda s: w_copy(opposite[s]).wait_recv())
        new = rwide.at[outer + 1]
        for side in range(2):
            for i in range(GHOST):
                at = pl.ds(base(i - GHOST if side == 0 else a + i), b)
                rows = slice(i * b, i * b + b)
                new[at, :] = stepped(
                    w[at, :], wxrecv[side, rows, :], lambda m: ixrecv[m, side, rows, :]
                )
                rows = slice(i * a, i * a + a)
                put_strip(new, side, i, stepped(
                    yrecv[side, i], wyrecv[side, rows, :], lambda m: iyrecv[m, side, rows, :]
                ))
        for s in range(4, 8):
            c = s - 4
            put_corner(new, s, stepped(
                crecv[c, :GHOST], wcrecv[c, :GHOST],
                lambda m: icrecv[c, GHOST * m : GHOST * m + GHOST, :],
            ))
        along = along - step * (onto - times(gram, as_row(y)))

    for k in range(OUTER + 1):
        most = slots.at[k, pl.ds(0, n - 1)]
        pltpu.make_async_copy(most, most, ps_sem.at[k]).wait()
    each(range(8), lambda s: ground_copy(s).wait_send())
    for m in range(nf):
        each(range(4), lambda s: field_copy(m, s).wait_send())
    each((0, 1, 4, 5, 6, 7), lambda s: all_do(deep_copies(s), "wait_send"))
    each(range(8), lambda s: w_copy(s).wait_send())
    for m in range(count):
        each(range(4), lambda s: image_copy(m, s).wait_send())
    each(range(4, 8), lambda s: image_copy(0, s).wait_send())


def store(sol_ref, res_ref, sol_out, res_out, sem):
    cps = [
        pltpu.make_async_copy(sol_ref, sol_out, sem.at[0]),
        pltpu.make_async_copy(res_ref, res_out, sem.at[1]),
    ]
    for cp in cps:
        cp.start()
    for cp in cps:
        cp.wait()


def solution(mesh):
    gxn, gyn = mesh.shape["gx"], mesh.shape["gy"]

    def local(right_side, first_guess, recycled, heights, ground_codes):
        a, b, nz = right_side.shape
        count = recycled.shape[0]
        field = jax.ShapeDtypeStruct((a * b, nz), F32)
        vm = pl.BlockSpec(memory_space=pltpu.VMEM)
        wide_f = pltpu.VMEM(((a + 2 * GHOST) * (b + 16), nz), F32)
        n = gxn * gyn
        hbm = pl.BlockSpec(memory_space=pltpu.HBM)
        dma = pltpu.SemaphoreType.DMA
        sol, res = pl.pallas_call(
            functools.partial(kernel, gxn, gyn, count, a, b),
            out_shape=(field, field),
            in_specs=[hbm] * 5,
            out_specs=(vm, vm),
            scratch_shapes=[
                pltpu.VMEM((a * b, nz), F32),
                pltpu.VMEM((a * b, nz), F32),
                pltpu.VMEM((count, a * b, nz), jnp.bfloat16),
                pltpu.VMEM((2, a, b), jnp.int32),
                pltpu.VMEM((8, 2, a, b), jnp.int32),
                pltpu.VMEM((count + 1, (a + 2) * (b + 16), nz), F32),
                pltpu.VMEM((count + 1, 2, b, nz), F32),
                pltpu.VMEM((count + 1, 2, a, nz), F32),
                pltpu.VMEM((count + 1, 2, a, nz), F32),
                pltpu.VMEM((OUTER,) + wide_f.shape, F32),
                pltpu.VMEM((2, GHOST, a, nz), F32),
                pltpu.VMEM((2, GHOST, a, nz), F32),
                pltpu.VMEM((4, 8, nz), F32),
                pltpu.VMEM((4, 8, nz), F32),
                wide_f,
                wide_f,
                pltpu.VMEM((SWEEPS,) + wide_f.shape, F32),
                wide_f,
                wide_f,
                pltpu.VMEM((OUTER, a * b, nz), F32),
                pltpu.VMEM((count, a * b, nz), F32),
                pltpu.VMEM((OUTER + 1, 1, nz), F32),
                pltpu.VMEM((OUTER + 1, n, 1, nz), F32),
                pltpu.VMEM((OUTER, a * b, nz), F32),
                pltpu.VMEM((2, GHOST * a, nz), F32),
                pltpu.VMEM((4, 8, nz), F32),
                pltpu.VMEM((2, GHOST * b, nz), F32),
                pltpu.VMEM((2, GHOST * a, nz), F32),
                pltpu.VMEM((4, 8, nz), F32),
                pltpu.VMEM((count, 2, GHOST * a, nz), F32),
                pltpu.VMEM((4, count * GHOST, nz), F32),
                pltpu.VMEM((count, 2, GHOST * b, nz), F32),
                pltpu.VMEM((count, 2, GHOST * a, nz), F32),
                pltpu.VMEM((4, count * GHOST, nz), F32),
                dma((4 + count,)),
                dma((8,)),
                dma((8,)),
                dma((count + 1, 4)),
                dma((count + 1, 4)),
                dma((8, GHOST)),
                dma((8, GHOST)),
                dma((OUTER + 1,)),
                dma((OUTER + 1,)),
                dma((8,)),
                dma((8,)),
                dma((count, 8)),
                dma((count, 8)),
                pltpu.SemaphoreType.REGULAR((max(gyn.bit_length(), 1), 2)),
            ],
            compiler_params=pltpu.CompilerParams(
                collective_id=0, has_side_effects=True, vmem_limit_bytes=32 * 2**20
            ),
        )(*[
            pltpu.with_memory_space_constraint(v, pltpu.HBM)
            for v in (
                right_side.reshape(a * b, nz),
                first_guess.reshape(a * b, nz),
                recycled.reshape(count, a * b, nz),
                heights,
                ground_codes,
            )
        ])
        sol, res = pl.pallas_call(
            store,
            out_shape=(field, field),
            in_specs=[vm] * 2,
            out_specs=(hbm, hbm),
            scratch_shapes=[dma((2,))],
            compiler_params=pltpu.CompilerParams(vmem_limit_bytes=4 * 2**20),
        )(sol, res)
        return sol.reshape(a, b, nz), res.reshape(a, b, nz)

    placed = (
        P("gx", "gy", None),
        P("gx", "gy", None),
        P(None, "gx", "gy", None),
        P("gx", "gy"),
        P("gx", "gy"),
    )
    return jax.shard_map(
        local,
        mesh=mesh,
        in_specs=placed,
        out_specs=(P("gx", "gy", None), P("gx", "gy", None)),
        check_vma=False,
    )
```

```python
import functools

import jax
import jax.numpy as jnp
from jax import lax
from jax.experimental import pallas as pl
from jax.experimental.pallas import tpu as pltpu
from jax.sharding import PartitionSpec as P

OUTER = 2
SWEEPS = 3
GHOST = SWEEPS
NEAR = 2

CENTER = 7.25
HALF = 6.75
SIGMA = 7.25 / 6.75

F32 = jnp.float32


def kernel(
    gxn, gyn, count, a, b,
    rs_hbm, fg_hbm, rec_hbm, h_hbm, code_hbm,
    sol_ref, res_ref,
    rs_ref, fg_ref, rec_ref, ground, near_ground,
    wide0, xrecv0, ysend0, yrecv0, rwide, ysend, yrecv, csend, crecv,
    fwide, diag, uwide, dwide, rem, cbuf, img, psend, slots,
    wown, wysend, wcsend, wxrecv, wyrecv, wcrecv, iysend, icsend, ixrecv, iyrecv, icrecv,
    in_sem, gs_sem, gr_sem, hs_sem, hr_sem, ds_sem, dr_sem, ps_sem, pr_sem, ws_sem, wr_sem, is_sem, ir_sem, known,
):
    lanes = 128
    S = b + 16
    n = gxn * gyn
    nf = count + 1
    gx = lax.axis_index("gx")
    gy = lax.axis_index("gy")
    me = gx * gyn + gy

    def at_dev(i, j):
        return dict(device_id={"gx": i, "gy": j}, device_id_type=pl.DeviceIdType.MESH)

    loads = [
        pltpu.make_async_copy(h_hbm, ground.at[0], in_sem.at[0]),
        pltpu.make_async_copy(code_hbm, ground.at[1], in_sem.at[1]),
        pltpu.make_async_copy(fg_hbm, fg_ref, in_sem.at[2]),
        pltpu.make_async_copy(rs_hbm, rs_ref, in_sem.at[3]),
    ] + [pltpu.make_async_copy(rec_hbm.at[m], rec_ref.at[m], in_sem.at[4 + m]) for m in range(count)]
    for cp in loads:
        cp.start()

    barrier = pltpu.get_barrier_semaphore()

    gis = [lax.rem(gx + i, gxn) for i in range(gxn)]
    gjs = [lax.rem(gy + j, gyn) for j in range(gyn)]

    greeters = -1
    for j in sorted(range(-NEAR, NEAR + 1), key=abs):
        inside = jnp.logical_and(gy + j >= 0, gy + j < gyn)
        greeters = greeters + jnp.where(inside, gxn, 0)

        @pl.when(inside)
        def _(j=j):
            for i in range(gxn):
                if i or j:
                    pl.semaphore_signal(barrier, inc=1, **at_dev(gis[i], gy + j))

    stages, reach = [], NEAR
    while reach < gyn - 1:
        stages.append(reach)
        reach *= 2

    def stage(k, act):
        for side, j in enumerate((-stages[k], stages[k])):
            @pl.when(jnp.logical_and(gy + j >= 0, gy + j < gyn))
            def _(side=side, j=j):
                if act == "signal":
                    pl.semaphore_signal(known.at[k, 1 - side], inc=1, **at_dev(gx, gy + j))
                else:
                    pl.semaphore_wait(known.at[k, side], 1)

    def base0(x):
        return S * (x + 1) + 8

    def base(x):
        return S * (x + GHOST) + 8

    def span(x):
        return pl.ds(S * (x + GHOST), S)

    lane8 = lax.broadcasted_iota(jnp.int32, (8, lanes), 1)
    sub8 = lax.broadcasted_iota(jnp.int32, (8, lanes), 0)
    row1 = lax.broadcasted_iota(jnp.int32, (1, lanes), 1)

    steps = ((-1, 0), (1, 0), (0, -1), (0, 1), (-1, -1), (-1, 1), (1, -1), (1, 1))
    opposite = [steps.index((-i, -j)) for i, j in steps]
    have, peers = [], []
    for i, j in steps:
        ok = None
        for at, size, by in ((gx, gxn, i), (gy, gyn, j)):
            if by:
                one = at > 0 if by < 0 else at < size - 1
                ok = one if ok is None else jnp.logical_and(ok, one)
        have.append(ok)
        peers.append(at_dev(gx + i, gy + j))

    def ground_copy(s):
        return pltpu.make_async_remote_copy(
            src_ref=ground, dst_ref=near_ground.at[opposite[s]],
            send_sem=gs_sem.at[s], recv_sem=gr_sem.at[opposite[s]], **peers[s],
        )

    def field_copy(m, s):
        w = wide0.at[m]
        src = (
            w.at[pl.ds(base0(0), b), :], w.at[pl.ds(base0(a - 1), b), :],
            ysend0.at[m, 0], ysend0.at[m, 1],
        )[s]
        dst = (
            xrecv0.at[m, 1], xrecv0.at[m, 0],
            yrecv0.at[m, 1], yrecv0.at[m, 0],
        )[s]
        return pltpu.make_async_remote_copy(
            src_ref=src, dst_ref=dst,
            send_sem=hs_sem.at[m, s], recv_sem=hr_sem.at[m, opposite[s]], **peers[s],
        )

    def send_to(s, src, dst, sends, recvs):
        return pltpu.make_async_remote_copy(
            src_ref=src, dst_ref=dst, send_sem=sends, recv_sem=recvs, **peers[s]
        )

    def deep_copies(s):
        w = rwide.at[0]
        if s < 2:
            pieces = [
                (
                    w.at[pl.ds(base(i if s == 0 else a - GHOST + i), b), :],
                    w.at[pl.ds(base(a + i if s == 0 else i - GHOST), b), :],
                )
                for i in range(GHOST)
            ]
        elif s < 4:
            pieces = [(ysend.at[s - 2], yrecv.at[3 - s])]
        else:
            pieces = [(csend.at[s - 4], crecv.at[opposite[s] - 4])]
        return [
            send_to(s, p, q, ds_sem.at[s, i], dr_sem.at[opposite[s], i])
            for i, (p, q) in enumerate(pieces)
        ]

    def face(field, s):
        return field.at[pl.ds(0 if s == 0 else (a - GHOST) * b, GHOST * b), :]

    def w_copy(s):
        if s < 2:
            src, dst = face(wown.at[0], s), wxrecv.at[1 - s]
        elif s < 4:
            src, dst = wysend.at[s - 2], wyrecv.at[3 - s]
        else:
            src, dst = wcsend.at[s - 4], wcrecv.at[opposite[s] - 4]
        return send_to(s, src, dst, ws_sem.at[s], wr_sem.at[opposite[s]])

    def image_copy(m, s):
        if s < 2:
            src, dst = face(img.at[m], s), ixrecv.at[m, 1 - s]
        elif s < 4:
            src, dst = iysend.at[m, s - 2], iyrecv.at[m, 3 - s]
        else:
            src, dst = icsend.at[s - 4], icrecv.at[opposite[s] - 4]
        return send_to(s, src, dst, is_sem.at[m, s], ir_sem.at[m, opposite[s]])

    def each(sides, act):
        for s in sides:
            @pl.when(have[s])
            def _(s=s):
                act(s)

    def all_do(cps, what):
        for cp in cps:
            getattr(cp, what)()

    zeros = jnp.zeros((b, lanes), F32)
    ones = jnp.ones((b, lanes), jnp.bfloat16)
    yi = lax.broadcasted_iota(jnp.int32, (S, b), 0)
    ji = lax.broadcasted_iota(jnp.int32, (S, b), 1)
    lane_f = lax.broadcasted_iota(jnp.int32, (S, lanes), 1).astype(F32)
    lane_s = lax.broadcasted_iota(jnp.int32, (S, lanes), 1)

    def spread(tables, i):
        left, mid, right = [jnp.broadcast_to(t[i : i + 1, :].astype(F32), (S, b)) for t in tables]
        pick = jnp.where(yi - 8 == ji, mid, 0.0)
        pick = jnp.where(yi == ji - (b - 8), left, pick)
        pick = jnp.where(yi - (b + 8) == ji, right, pick)
        return jnp.dot(pick.astype(jnp.bfloat16), ones, preferred_element_type=F32)

    def mask_row(x, trio, i):
        high = spread([t.at[0] for t in trio], i)
        code = spread([t.at[1] for t in trio], i)
        fwide[span(x), :] = jnp.where(lane_f >= high, 1.0, 0.0)
        bottom = jnp.where(code == 1.0, 0.5, 0.0) + jnp.where(code == 2.0, 2.0, 0.0)
        diag[span(x), :] = jnp.where(lane_s == 0, bottom, 0.0) + jnp.where(
            lane_s == lanes - 1, 1.0, 0.0
        )

    def fluid(x):
        return fwide[pl.ds(base(x), b), :]

    own_y = jnp.logical_and(lax.broadcasted_iota(jnp.int32, (S, lanes), 0) >= 8,
                            lax.broadcasted_iota(jnp.int32, (S, lanes), 0) < b + 8)

    def near(w, at, size):
        c = w[pl.ds(at, size), :]
        lane = lax.broadcasted_iota(jnp.int32, (size, lanes), 1)
        up = jnp.where(lane == lanes - 1, 0.0, pltpu.roll(c, lanes - 1, 1))
        down = jnp.where(lane == 0, 0.0, pltpu.roll(c, 1, 1))
        return (
            (w[pl.ds(at + S, size), :] + w[pl.ds(at - S, size), :])
            + (w[pl.ds(at + 1, size), :] + w[pl.ds(at - 1, size), :])
            + (up + down)
        )

    all_do(loads[:2], "wait")
    for x in (-1, a):
        fwide[span(x), :] = jnp.zeros((S, lanes), F32)
    for x in range(a):
        mask_row(x, (ground,) * 3, x)
        fwide[span(x), :] = jnp.where(own_y, fwide[span(x), :], 0.0)

    def set_diag(x):
        f = fwide[span(x), :]
        diag[span(x), :] = f * (near(fwide, S * (x + GHOST), S) + diag[span(x), :]) + (1.0 - f)

    def prepare(m):
        loads[2 if m == count else 4 + m].wait()
        w = wide0.at[m]
        for x in range(a):
            rows = slice(x * b, x * b + b)
            v = fg_ref[rows, :] if m == count else rec_ref[m, rows, :].astype(F32)
            w[pl.ds(base0(x), b), :] = fluid(x) * v
        ysend0[m, 0] = w[pl.ds(S + 8, a, stride=S), :]
        ysend0[m, 1] = w[pl.ds(S + 8 + b - 1, a, stride=S), :]

    order = [count] + list(range(count))
    early = order[: (nf + 1) // 2]
    for m in early:
        prepare(m)
    pl.semaphore_wait(barrier, greeters)
    each((4, 5, 6, 7, 2, 3, 0, 1), lambda s: ground_copy(s).start())
    for m in early:
        each((2, 3, 0, 1), lambda s: field_copy(m, s).start())
    for k in range(len(stages)):
        if k == 0:
            stage(k, "signal")
    for m in order[len(early) :]:
        prepare(m)
        each((2, 3, 0, 1), lambda s: field_copy(m, s).start())

    zeros_a = jnp.zeros((a, lanes), F32)
    for s in range(8):
        @pl.when(jnp.logical_not(have[s]))
        def _(s=s):
            near_ground[s, 0] = jnp.full((a, b), 255, jnp.int32)
            near_ground[s, 1] = jnp.zeros((a, b), jnp.int32)
            if s < 2:
                wxrecv[s] = jnp.zeros((GHOST * b, lanes), F32)
                for m in range(nf):
                    xrecv0[m, s] = zeros
                for m in range(count):
                    ixrecv[m, s] = jnp.zeros((GHOST * b, lanes), F32)
                for i in range(GHOST):
                    rwide[0, pl.ds(base(i - GHOST if s == 0 else a + i), b), :] = zeros
            elif s < 4:
                wyrecv[s - 2] = jnp.zeros((GHOST * a, lanes), F32)
                for m in range(nf):
                    yrecv0[m, s - 2] = zeros_a
                for m in range(count):
                    iyrecv[m, s - 2] = jnp.zeros((GHOST * a, lanes), F32)
                for i in range(GHOST):
                    yrecv[s - 2, i] = zeros_a
            else:
                crecv[s - 4] = jnp.zeros((8, lanes), F32)
                wcrecv[s - 4] = jnp.zeros((8, lanes), F32)
                icrecv[s - 4] = jnp.zeros((count * GHOST, lanes), F32)

    for m in range(nf):
        w = wide0.at[m]
        for x in (-1, a):
            w[pl.ds(base0(x), b), :] = zeros
        for y in (-1, b):
            w[pl.ds(base0(0) + y, a, stride=S), :] = zeros_a
    for x in range(a):
        set_diag(x)

    zero8 = jnp.zeros((8, lanes), F32)

    def tiles(v):
        return [v[i : i + 8] for i in range(0, v.shape[0], 8)]

    def total(v):
        return functools.reduce(jnp.add, tiles(v))

    table = {}
    loads[3].wait()
    waited = 0
    for turn, m in enumerate(order):
        sums = [zero8] * (m + 2)
        for x in range(a):
            rows = slice(x * b, x * b + b)
            dg = diag[pl.ds(base(x), b), :]
            flow = fluid(x) * near(wide0.at[m], base0(x), b)
            if m == count:
                res_ref[rows, :] = rs_ref[rows, :] - (dg * fg_ref[rows, :] - flow)
                continue
            v = dg * rec_ref[m, rows, :].astype(F32) - flow
            img[m, rows, :] = v
            if 0 < x < a - 1:
                inner = tiles(v)
                inner[0] = jnp.where(sub8 > 0, inner[0], 0.0)
                inner[-1] = jnp.where(sub8 < 7, inner[-1], 0.0)
                others = [img[q, rows, :] for q in range(m)] + [v, res_ref[rows, :]]
                sums = [
                    acc + functools.reduce(jnp.add, [i * j for i, j in zip(inner, tiles(o))])
                    for acc, o in zip(sums, others)
                ]
        if m < count:
            table[m] = sums
        if turn in (2, 6) and waited < len(stages):
            stage(waited, "wait")
            waited += 1
            if waited < len(stages):
                stage(waited, "signal")
    while waited < len(stages):
        stage(waited, "wait")
        waited += 1
        if waited < len(stages):
            stage(waited, "signal")

    each(range(8), lambda s: ground_copy(opposite[s]).wait_recv())
    for x in range(-GHOST, a + GHOST):
        if x < 0:
            trio, i = (near_ground.at[4], near_ground.at[0], near_ground.at[5]), a + x
        elif x < a:
            trio, i = (near_ground.at[2], ground, near_ground.at[3]), x
        else:
            trio, i = (near_ground.at[6], near_ground.at[1], near_ground.at[7]), x - a
        mask_row(x, trio, i)

    for x in range(1 - GHOST, a + GHOST - 1):
        set_diag(x)

    def column(items):
        rows = [jnp.sum(v, axis=0, keepdims=True) for v in items]
        if len(rows) < 8:
            rows.append(jnp.zeros((8 - len(rows), lanes), F32))
        return jnp.sum(jnp.concatenate(rows, axis=0), axis=1, keepdims=True)

    bits = ((0, 0), (0, 1), (1, 0))

    def corner_at(s, p, q):
        return p if steps[s][0] < 0 else a - 1 - p, q if steps[s][1] < 0 else b - 1 - q

    def take_strips(field, out):
        for i in range(GHOST):
            for side, y in enumerate((i, b - 1 - i)):
                out[side, i * a : (i + 1) * a, :] = field[pl.ds(y, a, stride=b), :]

    def image_strips(fields):
        for m in fields:
            take_strips(img.at[m], iysend.at[m])

    def share(fields):
        for m in fields:
            each((2, 3, 0, 1), lambda s: image_copy(m, s).start())

    first, second = count // 4, count * 3 // 4

    sub_a = lax.broadcasted_iota(jnp.int32, (a, lanes), 0)
    mid_a = jnp.logical_and(sub_a > 0, sub_a < a - 1)
    ends = [slice(x * b, x * b + b) for x in (0, a - 1)]
    strips = [pl.ds(y, a, stride=b) for y in (0, b - 1)]
    packed = zero8
    starts = []
    for m in order:
        each(range(4), lambda s: field_copy(m, opposite[s]).wait_recv())
        out = res_ref if m == count else img.at[m]
        sign = -1.0 if m == count else 1.0
        for i, (x, g) in enumerate(((0, -1), (a - 1, a))):
            add = fluid(g) * wide0[m, pl.ds(base0(x), b), :] - fluid(x) * xrecv0[m, i]
            out[ends[i], :] = out[ends[i], :] + sign * add
        for i, (y, g) in enumerate(((0, -1), (b - 1, b))):
            f_out = fwide[pl.ds(base(0) + g, a, stride=S), :]
            f_own = fwide[pl.ds(base(0) + y, a, stride=S), :]
            add = f_out * ysend0[m, i] - f_own * yrecv0[m, i]
            out[strips[i], :] = out[strips[i], :] + sign * add
        if m == count:
            continue
        sums = table[m]
        for part in ends + strips:
            v = img[m, part, :]
            others = [img[q, part, :] for q in range(m)] + [v, res_ref[part, :]]
            if part in strips:
                v = jnp.where(mid_a, v, 0.0)
            sums = [acc + total(v * o) for acc, o in zip(sums, others)]
        pair = jnp.logical_or(lane8 == 16 * sub8 + m, lane8 == 16 * m + sub8)
        packed = packed + jnp.where(jnp.logical_and(pair, sub8 <= m), column(sums[: m + 1]), 0.0)
        starts.append(sums[m + 1])
        if m < first:
            image_strips([m])
            share([m])
    packed = packed + jnp.where(lane8 == 16 * sub8 + count, column(starts), 0.0)

    far_first = sorted(
        [(i, j) for i in range(gxn) for j in range(gyn) if i or j],
        key=lambda t: (abs(t[1] - gyn // 2), abs(t[0] - gxn // 2)),
    )

    def sum_start(k, row):
        psend[k] = row
        slots[k, me] = row

        def send(gi, gj):
            pltpu.make_async_remote_copy(
                src_ref=psend.at[k], dst_ref=slots.at[k, me],
                send_sem=ps_sem.at[k], recv_sem=pr_sem.at[k], **at_dev(gi, gj),
            ).start()

        if n <= 64:
            for i, j in far_first:
                send(gis[i], gjs[j])
        else:
            def step(t, _):
                peer = lax.rem(me + t, n)
                send(peer // gyn, lax.rem(peer, gyn))
                return 0

            lax.fori_loop(1, n, step, 0)
    def sum_done(k):
        most = slots.at[k, pl.ds(0, n - 1)]
        pltpu.make_async_copy(most, most, pr_sem.at[k]).wait()
        return jnp.sum(slots[k], axis=0)

    def sum_sent(k):
        most = slots.at[k, pl.ds(0, n - 1)]
        pltpu.make_async_copy(most, most, ps_sem.at[k]).wait()

    def widened(v, size):
        return jnp.broadcast_to(v, (size, lanes))

    sum_start(0, jnp.sum(packed, axis=0, keepdims=True))
    image_strips(range(first, second))
    share(range(first, second))
    for s in range(4, 8):
        for i, (p, q) in enumerate(bits):
            x, y = corner_at(s, p, q)
            for m in range(count):
                icsend[s - 4, pl.ds(GHOST * m + i, 1), :] = img[m, pl.ds(x * b + y, 1), :]
    each(range(4, 8), lambda s: image_copy(0, s).start())
    image_strips(range(second, count))
    for s in range(4):
        csend[s] = zero8
        wcsend[s] = zero8
    row = sum_done(0)

    wrow = jnp.broadcast_to(row, (8, lanes))
    gram = zero8
    for m in range(count):
        moved = wrow if m == 0 else pltpu.roll(wrow, lanes - 16 * m, 1)
        gram = jnp.where(sub8 == m, moved, gram)
    cols = [jnp.broadcast_to(gram[:, k : k + 1], (8, lanes)) for k in range(count + 1)]
    start = cols[count]
    cols += [jnp.where(sub8 == k, 1.0, 0.0) for k in range(count)]
    for k in range(count):
        this = cols[k]
        scale = 1.0 / widened(this[k : k + 1], 8)
        for j in list(range(k + 1, count + 1)) + list(range(count + 1, count + 2 + k)):
            pivot = widened(cols[j][k : k + 1], 8) * scale
            cols[j] = jnp.where(sub8 == k, pivot, cols[j] - this * pivot)
    coef = cols[count]
    coeffs = [coef[m : m + 1] for m in range(count)]

    for x in range(a):
        rows = slice(x * b, x * b + b)
        res = res_ref[rows, :]
        for m in range(count):
            res = res - widened(coeffs[m], b) * img[m, rows, :]
        rwide[0, pl.ds(base(x), b), :] = res

    w = rwide.at[0]
    for i in range(GHOST):
        ysend[0, i] = w[pl.ds(base(0) + i, a, stride=S), :]
        ysend[1, i] = w[pl.ds(base(0) + b - 1 - i, a, stride=S), :]
    for s in range(4, 8):
        for i, (p, q) in enumerate(bits):
            x, y = corner_at(s, p, q)
            csend[s - 4, pl.ds(i, 1), :] = w[pl.ds(base(x) + y, 1), :]
    each((4, 5, 6, 7, 2, 3, 0, 1), lambda s: all_do(deep_copies(s), "start"))

    inverse = zero8
    for k in range(count):
        inverse = jnp.where(lane8 == k, cols[count + 1 + k], inverse)
    gram = jnp.where(lane8 < count, gram, 0.0)

    def times(matrix, row):
        return jnp.sum(matrix * row, axis=1, keepdims=True)

    def as_row(col):
        return jnp.sum(jnp.where(lane8 == sub8, col, 0.0), axis=0, keepdims=True)

    along = start - times(gram, as_row(coef))

    for x in range(a):
        rows = slice(x * b, x * b + b)
        sol = fg_ref[rows, :]
        for m in range(count):
            sol = sol + widened(coeffs[m], b) * rec_ref[m, rows, :].astype(F32)
        sol_ref[rows, :] = sol

    each((2, 3), lambda s: all_do(deep_copies(s), "wait_send"))
    share(range(second, count))
    each(range(8), lambda s: all_do(deep_copies(opposite[s]), "wait_recv"))

    def put_strip(w, side, i, v):
        y = -1 - i if side == 0 else b + i
        w[pl.ds(base(0) + y, a, stride=S), :] = v

    def put_corner(w, s, v):
        for i, (p, q) in enumerate(bits):
            x = -1 - p if steps[s][0] < 0 else a + p
            y = -1 - q if steps[s][1] < 0 else b + q
            w[pl.ds(base(x) + y, 1), :] = v[i : i + 1]

    for i in range(GHOST):
        for side in range(2):
            put_strip(w, side, i, yrecv[side, i])
    for s in range(4, 8):
        put_corner(w, s, crecv[s - 4])

    for outer in range(OUTER):
        last = outer + 1 == OUTER
        w = rwide.at[outer]
        for x in range(-GHOST, a + GHOST):
            uwide[0, span(x), :] = fwide[span(x), :] * (w[span(x), :] * (1.0 / CENTER))
        rho = 1.0 / SIGMA
        for sweep in range(SWEEPS):
            rho_new = 1.0 / (2.0 * SIGMA - rho)
            grow = SWEEPS - 1 - sweep
            for x in range(-grow, a + grow):
                at, size = (base(x), b) if grow == 0 else (S * (x + GHOST), S)
                rows = pl.ds(at, size)
                f = fwide[rows, :]
                old = w[rows, :] if sweep == 0 else rem[rows, :]
                d = old * (1.0 / CENTER) if sweep == 0 else dwide[rows, :]
                left = old - (diag[rows, :] * d - f * near(uwide.at[sweep], at, size))
                if 0 <= x < a:
                    own = slice(x * b, x * b + b)
                    mine = d if grow == 0 else d[8 : 8 + b]
                    cbuf[outer, own, :] = mine if sweep == 0 else cbuf[outer, own, :] + mine
                rem[rows, :] = left
                if sweep + 1 < SWEEPS:
                    d = (rho_new * rho) * d + (2.0 * rho_new / HALF) * left
                    dwide[rows, :] = d
                    uwide[sweep + 1, rows, :] = f * d
            rho = rho_new

        accs = [zero8] * (count + 2)
        for x in range(a):
            rows = slice(x * b, x * b + b)
            at = pl.ds(base(x), b)
            res = w[at, :]
            image = res - rem[at, :]
            wown[outer, rows, :] = image
            others = [img[m, rows, :] for m in range(count)] + [res, image]
            accs = [acc + total(image * o) for acc, o in zip(accs, others)]
        packed = (
            jnp.where(lane8 == sub8, column(accs[:count]), 0.0)
            + jnp.where(lane8 == sub8 + 16, column(accs[count:]), 0.0)
        )
        sum_start(1 + outer, jnp.sum(packed, axis=0, keepdims=True))
        if not last:
            take_strips(wown.at[outer], wysend)
            for s in range(4, 8):
                for i, (p, q) in enumerate(bits):
                    x, y = corner_at(s, p, q)
                    wcsend[s - 4, pl.ds(i, 1), :] = wown[outer, pl.ds(x * b + y, 1), :]
            each((4, 5, 6, 7, 2, 3, 0, 1), lambda s: w_copy(s).start())
            each(range(4), lambda s: all_do(
                [image_copy(m, opposite[s]) for m in range(count)], "wait_recv"))
            each(range(4, 8), lambda s: image_copy(0, opposite[s]).wait_recv())
        else:
            for x in range(a):
                earlier(x)
            for k in range(OUTER):
                sum_sent(k)
            each(range(8), lambda s: ground_copy(s).wait_send())
            each(range(4), lambda s: all_do([field_copy(m, s) for m in range(nf)], "wait_send"))
            each((0, 1, 4, 5, 6, 7), lambda s: all_do(deep_copies(s), "wait_send"))
            each(range(8), lambda s: w_copy(s).wait_send())
            each(range(4), lambda s: all_do([image_copy(m, s) for m in range(count)], "wait_send"))
            each(range(4, 8), lambda s: image_copy(0, s).wait_send())
        row = sum_done(1 + outer)

        onto_row = jnp.where(lane8 < count, jnp.broadcast_to(row, (8, lanes)), 0.0)
        y = times(inverse, onto_row)
        onto = jnp.sum(jnp.where(lane8 == sub8, onto_row, 0.0), axis=1, keepdims=True)
        numerator = row[:, 16:17] - jnp.sum(y * along, axis=0, keepdims=True)[:, 0:1]
        denominator = row[:, 17:18] - jnp.sum(y * onto, axis=0, keepdims=True)
        step = jnp.broadcast_to(numerator / denominator, (1, lanes))
        y = jnp.broadcast_to(y, (8, lanes))
        ys = [y[m : m + 1] for m in range(count)]

        def stepped(res, image, parts):
            size = res.shape[0]
            for m in range(count):
                image = image - widened(ys[m], size) * parts(m)
            return res - widened(step, size) * image

        for x in range(a):
            rows = slice(x * b, x * b + b)
            at = pl.ds(base(x), b)
            res = stepped(w[at, :], wown[outer, rows, :], lambda m: img[m, rows, :])
            if last:
                res_ref[rows, :] = res
            else:
                rwide[outer + 1, at, :] = res

        def solution_update(x, outer=outer, step=step, ys=ys):
            rows = slice(x * b, x * b + b)
            c = cbuf[outer, rows, :]
            for m in range(count):
                c = c - widened(ys[m], b) * rec_ref[m, rows, :].astype(F32)
            sol_ref[rows, :] = sol_ref[rows, :] + widened(step, b) * c

        if last:
            for x in range(a):
                solution_update(x)
            continue
        earlier = solution_update

        each(range(8), lambda s: w_copy(opposite[s]).wait_recv())
        new = rwide.at[outer + 1]
        for side in range(2):
            for i in range(GHOST):
                at = pl.ds(base(i - GHOST if side == 0 else a + i), b)
                rows = slice(i * b, i * b + b)
                new[at, :] = stepped(
                    w[at, :], wxrecv[side, rows, :], lambda m: ixrecv[m, side, rows, :]
                )
                rows = slice(i * a, i * a + a)
                put_strip(new, side, i, stepped(
                    yrecv[side, i], wyrecv[side, rows, :], lambda m: iyrecv[m, side, rows, :]
                ))
        for s in range(4, 8):
            c = s - 4
            put_corner(new, s, stepped(
                crecv[c, :GHOST], wcrecv[c, :GHOST],
                lambda m: icrecv[c, GHOST * m : GHOST * m + GHOST, :],
            ))
        along = along - step * (onto - times(gram, as_row(y)))

    sum_sent(OUTER)


def store(sol_ref, res_ref, sol_out, res_out, sem):
    cps = [
        pltpu.make_async_copy(sol_ref, sol_out, sem.at[0]),
        pltpu.make_async_copy(res_ref, res_out, sem.at[1]),
    ]
    for cp in cps:
        cp.start()
    for cp in cps:
        cp.wait()


def solution(mesh):
    gxn, gyn = mesh.shape["gx"], mesh.shape["gy"]

    def local(right_side, first_guess, recycled, heights, ground_codes):
        a, b, nz = right_side.shape
        count = recycled.shape[0]
        field = jax.ShapeDtypeStruct((a * b, nz), F32)
        vm = pl.BlockSpec(memory_space=pltpu.VMEM)
        wide_f = pltpu.VMEM(((a + 2 * GHOST) * (b + 16), nz), F32)
        n = gxn * gyn
        hbm = pl.BlockSpec(memory_space=pltpu.HBM)
        dma = pltpu.SemaphoreType.DMA
        sol, res = pl.pallas_call(
            functools.partial(kernel, gxn, gyn, count, a, b),
            out_shape=(field, field),
            in_specs=[hbm] * 5,
            out_specs=(vm, vm),
            scratch_shapes=[
                pltpu.VMEM((a * b, nz), F32),
                pltpu.VMEM((a * b, nz), F32),
                pltpu.VMEM((count, a * b, nz), jnp.bfloat16),
                pltpu.VMEM((2, a, b), jnp.int32),
                pltpu.VMEM((8, 2, a, b), jnp.int32),
                pltpu.VMEM((count + 1, (a + 2) * (b + 16), nz), F32),
                pltpu.VMEM((count + 1, 2, b, nz), F32),
                pltpu.VMEM((count + 1, 2, a, nz), F32),
                pltpu.VMEM((count + 1, 2, a, nz), F32),
                pltpu.VMEM((OUTER,) + wide_f.shape, F32),
                pltpu.VMEM((2, GHOST, a, nz), F32),
                pltpu.VMEM((2, GHOST, a, nz), F32),
                pltpu.VMEM((4, 8, nz), F32),
                pltpu.VMEM((4, 8, nz), F32),
                wide_f,
                wide_f,
                pltpu.VMEM((SWEEPS,) + wide_f.shape, F32),
                wide_f,
                wide_f,
                pltpu.VMEM((OUTER, a * b, nz), F32),
                pltpu.VMEM((count, a * b, nz), F32),
                pltpu.VMEM((OUTER + 1, 1, nz), F32),
                pltpu.VMEM((OUTER + 1, n, 1, nz), F32),
                pltpu.VMEM((OUTER, a * b, nz), F32),
                pltpu.VMEM((2, GHOST * a, nz), F32),
                pltpu.VMEM((4, 8, nz), F32),
                pltpu.VMEM((2, GHOST * b, nz), F32),
                pltpu.VMEM((2, GHOST * a, nz), F32),
                pltpu.VMEM((4, 8, nz), F32),
                pltpu.VMEM((count, 2, GHOST * a, nz), F32),
                pltpu.VMEM((4, count * GHOST, nz), F32),
                pltpu.VMEM((count, 2, GHOST * b, nz), F32),
                pltpu.VMEM((count, 2, GHOST * a, nz), F32),
                pltpu.VMEM((4, count * GHOST, nz), F32),
                dma((4 + count,)),
                dma((8,)),
                dma((8,)),
                dma((count + 1, 4)),
                dma((count + 1, 4)),
                dma((8, GHOST)),
                dma((8, GHOST)),
                dma((OUTER + 1,)),
                dma((OUTER + 1,)),
                dma((8,)),
                dma((8,)),
                dma((count, 8)),
                dma((count, 8)),
                pltpu.SemaphoreType.REGULAR((max(gyn.bit_length(), 1), 2)),
            ],
            compiler_params=pltpu.CompilerParams(
                collective_id=0, has_side_effects=True, vmem_limit_bytes=32 * 2**20
            ),
        )(*[
            pltpu.with_memory_space_constraint(v, pltpu.HBM)
            for v in (
                right_side.reshape(a * b, nz),
                first_guess.reshape(a * b, nz),
                recycled.reshape(count, a * b, nz),
                heights,
                ground_codes,
            )
        ])
        sol, res = pl.pallas_call(
            store,
            out_shape=(field, field),
            in_specs=[vm] * 2,
            out_specs=(hbm, hbm),
            scratch_shapes=[dma((2,))],
            compiler_params=pltpu.CompilerParams(vmem_limit_bytes=4 * 2**20),
        )(sol, res)
        return sol.reshape(a, b, nz), res.reshape(a, b, nz)

    placed = (
        P("gx", "gy", None),
        P("gx", "gy", None),
        P(None, "gx", "gy", None),
        P("gx", "gy"),
        P("gx", "gy"),
    )
    return jax.shard_map(
        local,
        mesh=mesh,
        in_specs=placed,
        out_specs=(P("gx", "gy", None), P("gx", "gy", None)),
        check_vma=False,
    )
```
